256 devices in a mesh: ctx: 32 (over z, x), batch: 8 (over y, core).
Axes of the slice: x: 4, y: 4, z: 8, core: 2. Of those that a mesh axis runs over, the one named last changes fastest.
Arguments:
- kda_query: bfloat16 [32768, 2048], P(('batch', 'ctx')), parts along dimension 0, may hold values from -6 to 6
- kda_key: bfloat16 [32768, 2048], P(('batch', 'ctx')), parts along dimension 0, may hold values from -6 to 6
- kda_value: bfloat16 [32768, 2048], P(('batch', 'ctx')), parts along dimension 0, may hold values from -6 to 6
- log_decay: bfloat16 [32768, 2048], P(('batch', 'ctx')), parts along dimension 0, may hold values from -2 to 0
- write_rate: float32 [32768, 16], P(('batch', 'ctx')), parts along dimension 0, may hold values from 0.01 to 0.9
- mla_query: bfloat16 [32768, 3072], P(('batch', 'ctx')), parts along dimension 0, may hold values from -8 to 8
- latents: bfloat16 [32768, 576], P(('batch', 'ctx')), parts along dimension 0, may hold values from -8 to 8
- key_up: bfloat16 [512, 2048], replicated, may hold values from -0.25 to 0.25
- value_up: bfloat16 [512, 2048], replicated, may hold values from -0.25 to 0.25
- doc_lengths: int32 [64], P('batch'), parts along dimension 0, may hold values from 1 to 2048, 4096 in all
Outputs:
- kda_out: bfloat16 [32768, 2048], P(('batch', 'ctx')), parts along dimension 0
- mla_out: bfloat16 [32768, 2048], P(('batch', 'ctx')), parts along dimension 0
The draws below stay inside these ranges and needn't reach their ends.
There are 8 independent parts, one for each index of `batch`. The reference program is written for one: setup_inputs(seed, part) draws one part's arguments, and reference() takes and returns one part's arrays. A program takes and returns all parts, laid end to end along the dimension named above; an argument that names none is the same for every part. Nothing has to cross between parts.
Inputs may be any that keep to these rules, and one draw needn't show every extreme that they name: `doc_lengths`: 8 lengths of the documents of one context in order; they sum to 4096 and the longest is exactly 2048.
All inputs are finite; a program needn't handle non-finite values.
Results may differ from the reference program's by a relative error of at most 0.009.
Values may be sent and summed in bfloat16 or wider, within the bound.
A program may use at most 192 MiB of HBM per device.

```python
import math
import jax
import jax.numpy as jnp
import numpy as np
from jax import lax

HEADS = 16
DK = 128
DV = 128
NOPE = 128
ROPE = 64
LATENT = 512
BLOCK = 64
NDOCS = 8
TOK_DEV = 128
CONTEXT_SIZE = 4096


def loguniform_draw(key, shape_all, lowest, highest):
    return jnp.exp(jax.random.uniform(key, shape_all, jnp.float32, jnp.log(lowest), jnp.log(highest)))


def draw_latents(key, part):
    shape_all = (CONTEXT_SIZE, LATENT + ROPE)
    base = jnp.clip(jax.random.normal(jax.random.fold_in(key, 1), shape_all, jnp.float32), -6.0, 6.0)
    return base.astype(jnp.bfloat16)


def draw_mla_query(key, part):
    shape_all = (CONTEXT_SIZE, HEADS, NOPE + ROPE)
    base = jnp.clip(jax.random.normal(jax.random.fold_in(key, 3), shape_all, jnp.float32), -6.0, 6.0)
    return base.reshape(CONTEXT_SIZE, HEADS * (NOPE + ROPE)).astype(jnp.bfloat16)


def draw_log_decay(key, part):
    head_bits = jax.random.bernoulli(jax.random.fold_in(key, 21), 0.5, (HEADS, 1))
    slow_rate = loguniform_draw(jax.random.fold_in(key, 22), (HEADS, DK), 0.1 / CONTEXT_SIZE, 1.0 / CONTEXT_SIZE)
    fast_rate = loguniform_draw(jax.random.fold_in(key, 23), (HEADS, DK), 1.0 / CONTEXT_SIZE, 1.0 / 25.0)
    channel_decay_rate = jnp.where(head_bits, slow_rate, fast_rate)
    approximate = jax.random.uniform(jax.random.fold_in(key, 25), (CONTEXT_SIZE, HEADS, DK), jnp.float32, 0.5, 1.5)
    segment_factor = loguniform_draw(jax.random.fold_in(key, 26), (CONTEXT_SIZE // TOK_DEV, 1, 1), 0.5, 2.0)
    segment_factor = jnp.repeat(segment_factor, TOK_DEV, axis=0)
    spike_positions = jax.random.randint(jax.random.fold_in(key, 27), (6,), 0, CONTEXT_SIZE)
    spike_lengths = jnp.log(jax.random.uniform(jax.random.fold_in(key, 28), (6,), jnp.float32, 0.5, 0.8))
    match_count = (jnp.arange(CONTEXT_SIZE)[:, None] == spike_positions[None, :]).astype(jnp.float32)
    spike_run = jnp.sum(match_count * spike_lengths[None, :], axis=1)
    logarithm_decay = -channel_decay_rate[None] * approximate * segment_factor + spike_run[:, None, None]
    return logarithm_decay.reshape(CONTEXT_SIZE, HEADS * DK).astype(jnp.bfloat16)


def draw_write_rate(key, part):
    head_base = loguniform_draw(jax.random.fold_in(key, 31), (1, HEADS), 0.02, 0.6)
    approximate = jax.random.uniform(jax.random.fold_in(key, 32), (CONTEXT_SIZE, HEADS), jnp.float32, 0.5, 1.5)
    return (head_base * approximate).astype(jnp.float32)


def level_of(stream_key, dims, cuts, smallest, high):
    loudness = 1.0
    for dim, parts in cuts:
        heights = jax.random.uniform(jax.random.fold_in(jax.random.fold_in(stream_key, 6), dim), (parts,), jnp.float32, smallest / len(cuts), high / len(cuts))
        loudness = loudness * jnp.repeat(jnp.exp(heights), dims[dim] // parts).reshape((-1,) + (1,) * (len(dims) - 1 - dim))
    return loudness


def length_profile(amount, total, limit, lean):
    weights = [(1 << 20) // math.isqrt(rank ** lean) + 1 for rank in range(2, amount + 1)]
    spare, counts = total - limit - (amount - 1), [1] * (amount - 1)
    while spare > 0:
        candidates = [i for i in range(amount - 1) if counts[i] < limit]
        mass, remaining = sum([weights[i] for i in candidates]), spare
        for i in candidates:
            more = min(limit - counts[i], max(1, remaining * weights[i] // mass), spare)
            counts[i] = counts[i] + more
            spare = spare - more
    return np.array([limit] + counts)


def ragged(key, number_of, total, bound, lean):
    if number_of == 2:
        one = jax.random.randint(key, (), max(1, total - bound), min(bound, total - 1) + 1)
        return jnp.stack([one, total - one])
    tallies = jnp.asarray(length_profile(number_of, total, bound, lean), jnp.int32)
    couples = (number_of - 1) // 2
    source_of, receiver = tallies[1:1 + 2 * couples:2], tallies[2:2 + 2 * couples:2]
    room = jnp.minimum(source_of - 1, bound - receiver)
    shifted = jax.random.randint(jax.random.fold_in(key, 1), (couples,), 0, 1 << 20) % (room + 1)
    tallies = tallies.at[1:1 + 2 * couples:2].set(source_of - shifted).at[2:2 + 2 * couples:2].set(receiver + shifted)
    return tallies[jax.random.permutation(jax.random.fold_in(key, 2), number_of)]


def normal_values(rng, shape, scale, reach, split=(), kind=jnp.bfloat16):
    array = jax.random.normal(rng, shape, jnp.float32) * scale
    if len(split) > 0:
        array = level_of(rng, shape, split, -0.22, 0.18) * array
    return jnp.clip(array, min=-reach, max=reach).astype(kind)


def setup_inputs(seed: int = 0, part: int = 0) -> dict:
    splits = jax.random.split(jax.random.key(seed), 11)
    part_splits = jax.random.split(jax.random.fold_in(splits[10], part), 11)
    kda_query = normal_values(part_splits[0], (CONTEXT_SIZE, HEADS * DK), 1.0, 6.0, ((0, 32),))
    kda_key = normal_values(part_splits[1], (CONTEXT_SIZE, HEADS * DK), 1.0, 6.0, ((0, 32),))
    kda_value = normal_values(part_splits[2], (CONTEXT_SIZE, HEADS * DV), 1.0, 6.0, ((0, 32),))
    log_decay = draw_log_decay(jax.random.fold_in(jax.random.fold_in(splits[10], part), 71), part)
    write_rate = draw_write_rate(jax.random.fold_in(jax.random.fold_in(splits[10], part), 71), part)
    mla_query = draw_mla_query(jax.random.fold_in(jax.random.fold_in(splits[10], part), 71), part)
    latents = draw_latents(jax.random.fold_in(jax.random.fold_in(splits[10], part), 71), part)
    key_up = normal_values(splits[7], (LATENT, HEADS * NOPE), LATENT ** -0.5, 0.25)
    value_up = normal_values(splits[8], (LATENT, HEADS * DV), LATENT ** -0.5, 0.25)
    doc_lengths = ragged(part_splits[9], NDOCS, CONTEXT_SIZE, CONTEXT_SIZE // 2, 2).astype(jnp.int32)
    return {"kda_query": kda_query, "kda_key": kda_key, "kda_value": kda_value, "log_decay": log_decay, "write_rate": write_rate, "mla_query": mla_query, "latents": latents, "key_up": key_up, "value_up": value_up, "doc_lengths": doc_lengths}


PRECISE_PRODUCT = lax.Precision.HIGHEST

def unit_rows(values):
    return values * lax.rsqrt(lax.optimization_barrier(jnp.sum(values * values, axis=-1, keepdims=True)) + 1e-06)

def doc_of(positions, doc_starts):
    match_count = (doc_starts[None, :] <= positions[:, None]).astype(jnp.int32)
    return (lax.optimization_barrier(jnp.sum(match_count, axis=1)) - 1).astype(jnp.int32)

def unit_lower_inverse(strictly_lower):
    length = strictly_lower.shape[-1]
    identity = jnp.eye(length, dtype=jnp.float32)[None]
    result = identity - strictly_lower
    power_term = strictly_lower
    for level_index in range(length.bit_length() - 2):
        power_term = jnp.einsum('hij,hjk->hik', power_term, power_term, precision=PRECISE_PRODUCT)
        result = jnp.einsum('hij,hjk->hik', result, identity + power_term, precision=PRECISE_PRODUCT)
    return result

def block_terms(query_unit, keyvec, valvec, logarithm_decay, write_gain, docids, prevdoc):
    length = docids.shape[0]
    cumulative = jnp.cumsum(logarithm_decay, axis=0)
    growth = jnp.exp(cumulative)
    key_plus = keyvec * growth
    key_minus = keyvec * jnp.exp(-cumulative)
    query_plus = query_unit * growth
    places = jnp.arange(length)
    same_doc = docids[:, None] == docids[None, :]
    strict = (places[:, None] > places[None, :]) & same_doc
    causal = (places[:, None] >= places[None, :]) & same_doc
    follow = (docids == prevdoc).astype(jnp.float32)
    inner_prod = jnp.einsum('thk,shk->hts', key_plus, key_minus, precision=PRECISE_PRODUCT)
    strictly_lower = jnp.where(strict[None], inner_prod, 0.0) * jnp.transpose(write_gain)[:, :, None]
    inverse = unit_lower_inverse(strictly_lower)
    value_rhs = jnp.transpose(valvec * write_gain[:, :, None], (1, 0, 2))
    key_rhs = jnp.transpose(key_plus * (write_gain * follow[:, None])[:, :, None], (1, 0, 2))
    value_solution = jnp.einsum('hts,hsv->htv', inverse, value_rhs, precision=PRECISE_PRODUCT)
    solved_key = jnp.einsum('hts,hsk->htk', inverse, key_rhs, precision=PRECISE_PRODUCT)
    mixing = jnp.where(causal[None], jnp.einsum('thk,shk->hts', query_plus, key_minus, precision=PRECISE_PRODUCT), 0.0)
    local_output = jnp.einsum('hts,hsv->htv', mixing, value_solution, precision=PRECISE_PRODUCT)
    query_effective = jnp.transpose(query_plus * follow[:, None, None], (1, 0, 2)) - jnp.einsum('hts,hsk->htk', mixing, solved_key, precision=PRECISE_PRODUCT)
    last_doc = (docids == docids[length - 1]).astype(jnp.float32)
    key_trailing = keyvec * jnp.exp(cumulative[length - 1][None] - cumulative) * last_doc[:, None, None]
    growth_last = growth[length - 1]
    diagonal_map = growth_last[:, :, None] * jnp.eye(keyvec.shape[2], dtype=jnp.float32)[None]
    handed_operator = follow[length - 1] * diagonal_map - jnp.einsum('shk,hsj->hkj', key_trailing, solved_key, precision=PRECISE_PRODUCT)
    handed_update = jnp.einsum('omt,mor->mtr', key_trailing, value_solution, precision=PRECISE_PRODUCT)
    return (local_output, query_effective, handed_operator, handed_update)

def kda_layer(kda_query, kda_key, kda_value, log_decay, write_rate, docids):
    total_rows = kda_query.shape[0]
    head_count = write_rate.shape[1]
    query_unit = unit_rows(kda_query.astype(jnp.float32).reshape(total_rows, head_count, -1))
    keyvec = unit_rows(kda_key.astype(jnp.float32).reshape(total_rows, head_count, -1))
    valvec = kda_value.astype(jnp.float32).reshape(total_rows, head_count, -1)
    logarithm_decay = log_decay.astype(jnp.float32).reshape(total_rows, head_count, -1)
    blocks = total_rows // BLOCK
    prevdocs = jnp.concatenate([jnp.full((1,), -1, jnp.int32), docids[:-1]])[::BLOCK]

    def shaped(values):
        return values.reshape((blocks, BLOCK) + values.shape[1:])

    def advance(handed_forward, inputs):
        local_output, query_effective, handed_operator, handed_update = block_terms(*inputs)
        final_output = local_output + jnp.einsum('cor,crm->com', query_effective, handed_forward, precision=PRECISE_PRODUCT)
        handed_forward = jnp.einsum('ytn,yne->yte', handed_operator, handed_forward, precision=PRECISE_PRODUCT) + handed_update
        return (handed_forward, final_output)
    initial = jnp.zeros((head_count, keyvec.shape[2], valvec.shape[2]), jnp.float32)
    xs_all = (shaped(query_unit), shaped(keyvec), shaped(valvec), shaped(logarithm_decay), shaped(write_rate.astype(jnp.float32)), shaped(docids), prevdocs)
    _, outputs = lax.scan(advance, initial, xs_all)
    return jnp.transpose(outputs, (0, 2, 1, 3)).reshape(total_rows, -1).astype(jnp.bfloat16)

def mla_layer(mla_query, latents, key_up, value_up, docids):
    total_rows = latents.shape[0]
    head_count = key_up.shape[1] // NOPE
    latent_part = latents[:, :LATENT]
    keys_nope = jnp.dot(latent_part, key_up, preferred_element_type=jnp.float32).astype(jnp.bfloat16)
    values = jnp.dot(latent_part, value_up, preferred_element_type=jnp.float32).astype(jnp.bfloat16)
    keys_wide = keys_nope.astype(jnp.float32).reshape(total_rows, head_count, NOPE)
    values_wide = values.astype(jnp.float32).reshape(total_rows, head_count, -1)
    rope_keys = latents[:, LATENT:].astype(jnp.float32)
    queries = mla_query.astype(jnp.float32).reshape(total_rows, head_count, NOPE + ROPE)
    score_scale = 1.0 / math.sqrt(NOPE + ROPE)
    positions = jnp.arange(total_rows, dtype=jnp.int32)
    blocks = total_rows // TOK_DEV

    def attend(inputs):
        query_block, place_block, doc_block = inputs
        scores = jnp.einsum('thd,shd->hts', query_block[:, :, :NOPE], keys_wide)
        scores = (scores + jnp.einsum('thr,sr->hts', query_block[:, :, NOPE:], rope_keys)) * score_scale
        allowed = (positions[None, :] <= place_block[:, None]) & (docids[None, :] == doc_block[:, None])
        masked = jnp.where(allowed[None], scores, -1e+30)
        row_max = lax.optimization_barrier(jnp.max(masked, axis=2, keepdims=True))
        weights = jnp.where(allowed[None], jnp.exp(masked - row_max), 0.0)
        row_total = lax.optimization_barrier(jnp.sum(weights, axis=2))
        rounded = lax.optimization_barrier(weights.astype(jnp.bfloat16)).astype(jnp.float32)
        summed = jnp.einsum('hts,shv->thv', rounded, values_wide)
        return (summed / jnp.transpose(row_total)[:, :, None]).astype(jnp.bfloat16)
    outputs = lax.map(attend, (queries.reshape(blocks, TOK_DEV, head_count, NOPE + ROPE), positions.reshape(blocks, TOK_DEV), docids.reshape(blocks, TOK_DEV)))
    return outputs.reshape(total_rows, -1)

def reference(kda_query, kda_key, kda_value, log_decay, write_rate, mla_query, latents, key_up, value_up, doc_lengths):
    doc_starts = (jnp.cumsum(doc_lengths) - doc_lengths).astype(jnp.int32)
    positions = jnp.arange(latents.shape[0], dtype=jnp.int32)
    docids = doc_of(positions, doc_starts)
    kda_out = kda_layer(kda_query, kda_key, kda_value, log_decay, write_rate, docids)
    mla_out = mla_layer(mla_query, latents, key_up, value_up, docids)
    return (kda_out, mla_out)
```

```python
import math

import jax
import jax.numpy as jnp
from jax import lax
from jax.sharding import PartitionSpec as P

NOPE = 128
ROPE = 64
LATENT = 512
BLOCK = 64


PRECISE_PRODUCT = lax.Precision.HIGHEST


def prefix(array, axis, join, neutral):
    place = lax.axis_index(axis)
    gathered = jax.tree.map(
        lambda a, kind: lax.all_gather(a.astype(kind), axis),
        array,
        jax.tree.map(lambda a: jnp.bfloat16 if a.dtype == jnp.float32 else a.dtype, array),
    )
    state = jax.tree.map(lambda a, e: jnp.zeros_like(a) + jnp.asarray(e, a.dtype), array, neutral)

    def one(step, state):
        return join(
            state,
            jax.tree.map(
                lambda a, own: lax.dynamic_index_in_dim(a, step, 0, False).astype(own.dtype),
                gathered,
                array,
            ),
        )

    return lax.fori_loop(0, place, one, state)


def shifted(block, axis, distance):
    devices = range(lax.axis_size(axis))
    route = [(i - distance, i) for i in devices if i - distance in devices]
    return lax.ppermute(block, axis, route)


def unit_rows(values):
    return values * lax.rsqrt(jnp.sum(values * values, axis=-1, keepdims=True) + 1e-06)


def doc_of(positions, doc_starts):
    match_count = (doc_starts[None, :] <= positions[:, None]).astype(jnp.int32)
    return jnp.sum(match_count, axis=1) - 1


def unit_lower_inverse(strictly_lower):
    length = strictly_lower.shape[-1]
    identity = jnp.eye(length, dtype=jnp.float32)[None]
    result = identity - strictly_lower
    power_term = strictly_lower
    for level_index in range(length.bit_length() - 2):
        power_term = jnp.einsum("hij,hjk->hik", power_term, power_term, precision=PRECISE_PRODUCT)
        result = jnp.einsum(
            "hij,hjk->hik", result, identity + power_term, precision=PRECISE_PRODUCT
        )
    return result


def block_terms(query_unit, keyvec, valvec, logarithm_decay, write_gain, docids, prevdoc):
    length = docids.shape[0]
    cumulative = jnp.cumsum(logarithm_decay, axis=0)
    growth = jnp.exp(cumulative)
    key_plus = keyvec * growth
    key_minus = keyvec * jnp.exp(-cumulative)
    query_plus = query_unit * growth
    places = jnp.arange(length)
    same_doc = docids[:, None] == docids[None, :]
    strict = (places[:, None] > places[None, :]) & same_doc
    causal = (places[:, None] >= places[None, :]) & same_doc
    follow = (docids == prevdoc).astype(jnp.float32)
    inner_prod = jnp.einsum("thk,shk->hts", key_plus, key_minus, precision=PRECISE_PRODUCT)
    strictly_lower = (
        jnp.where(strict[None], inner_prod, 0.0) * jnp.transpose(write_gain)[:, :, None]
    )
    inverse = unit_lower_inverse(strictly_lower)
    value_rhs = jnp.transpose(valvec * write_gain[:, :, None], (1, 0, 2))
    key_rhs = jnp.transpose(key_plus * (write_gain * follow[:, None])[:, :, None], (1, 0, 2))
    value_solution = jnp.einsum("hts,hsv->htv", inverse, value_rhs, precision=PRECISE_PRODUCT)
    solved_key = jnp.einsum("hts,hsk->htk", inverse, key_rhs, precision=PRECISE_PRODUCT)
    mixing = jnp.where(
        causal[None],
        jnp.einsum("thk,shk->hts", query_plus, key_minus, precision=PRECISE_PRODUCT),
        0.0,
    )
    local_output = jnp.einsum("hts,hsv->htv", mixing, value_solution, precision=PRECISE_PRODUCT)
    query_effective = jnp.transpose(query_plus * follow[:, None, None], (1, 0, 2)) - jnp.einsum(
        "hts,hsk->htk", mixing, solved_key, precision=PRECISE_PRODUCT
    )
    last_doc = (docids == docids[length - 1]).astype(jnp.float32)
    key_trailing = (
        keyvec * jnp.exp(cumulative[length - 1][None] - cumulative) * last_doc[:, None, None]
    )
    growth_last = growth[length - 1]
    diagonal_map = growth_last[:, :, None] * jnp.eye(keyvec.shape[2], dtype=jnp.float32)[None]
    handed_operator = follow[length - 1] * diagonal_map - jnp.einsum(
        "shk,hsj->hkj", key_trailing, solved_key, precision=PRECISE_PRODUCT
    )
    handed_update = jnp.einsum(
        "omt,mor->mtr", key_trailing, value_solution, precision=PRECISE_PRODUCT
    )
    return (local_output, query_effective, handed_operator, handed_update)


def compose(prior_slab, successor_slab):
    joined_map = jnp.einsum(
        "hkj,hjl->hkl", successor_slab[0], prior_slab[0], precision=PRECISE_PRODUCT
    )
    combined_increment = (
        jnp.einsum("ytn,yne->yte", successor_slab[0], prior_slab[1], precision=PRECISE_PRODUCT)
        + successor_slab[1]
    )
    return (joined_map, combined_increment)


def local(
    kda_query,
    kda_key,
    kda_value,
    log_decay,
    write_rate,
    mla_query,
    latents,
    key_up,
    value_up,
    doc_lengths,
):
    slab_rows = latents.shape[0]
    head_count = write_rate.shape[1]
    first_row = lax.axis_index("ctx") * slab_rows
    doc_starts = jnp.cumsum(doc_lengths) - doc_lengths
    positions = first_row + jnp.arange(slab_rows, dtype=jnp.int32)
    docids = doc_of(positions, doc_starts)
    query_unit = unit_rows(kda_query.astype(jnp.float32).reshape(slab_rows, head_count, -1))
    keyvec = unit_rows(kda_key.astype(jnp.float32).reshape(slab_rows, head_count, -1))
    valvec = kda_value.astype(jnp.float32).reshape(slab_rows, head_count, -1)
    logarithm_decay = log_decay.astype(jnp.float32).reshape(slab_rows, head_count, -1)
    block_count = slab_rows // BLOCK
    prevdocs = doc_of(first_row + jnp.arange(block_count, dtype=jnp.int32) * BLOCK - 1, doc_starts)

    def shaped(values):
        return values.reshape((block_count, BLOCK) + values.shape[1:])

    block_outs = jax.vmap(block_terms)(
        shaped(query_unit),
        shaped(keyvec),
        shaped(valvec),
        shaped(logarithm_decay),
        shaped(write_rate),
        shaped(docids),
        prevdocs,
    )
    key_dim = keyvec.shape[2]
    value_dim = valvec.shape[2]
    identity_map = jnp.broadcast_to(
        jnp.eye(key_dim, dtype=jnp.float32)[None], (head_count, key_dim, key_dim)
    )
    zero_add = jnp.zeros((head_count, key_dim, value_dim), jnp.float32)

    def advance_block(prefix_pair, block_item):
        map_before, update_from_prior = prefix_pair
        local_output, query_effective, handed_operator, handed_update = block_item
        eff_now = jnp.einsum("htk,hkj->htj", query_effective, map_before, precision=PRECISE_PRODUCT)
        output_current = local_output + jnp.einsum(
            "cor,crm->com", query_effective, update_from_prior, precision=PRECISE_PRODUCT
        )
        map_after = jnp.einsum(
            "hkj,hjl->hkl", handed_operator, map_before, precision=PRECISE_PRODUCT
        )
        increment_later = (
            jnp.einsum(
                "ytn,yne->yte", handed_operator, update_from_prior, precision=PRECISE_PRODUCT
            )
            + handed_update
        )
        return ((map_after, increment_later), (eff_now, output_current))

    slab_pair, per_block = lax.scan(advance_block, (identity_map, zero_add), block_outs)
    effective_everything, output_everything = per_block
    carried_in = incoming_state(slab_pair, slab_rows)
    delta_attention_complete = output_everything + jnp.einsum(
        "enzx,nxu->enzu", effective_everything, carried_in, precision=PRECISE_PRODUCT
    )
    kda_out = (
        jnp.transpose(delta_attention_complete, (0, 2, 1, 3))
        .reshape(slab_rows, -1)
        .astype(jnp.bfloat16)
    )
    mla_out = latent_attention(
        mla_query, latents, key_up, value_up, positions, docids, doc_starts, head_count
    )
    return (kda_out, mla_out)


def window_slabs_of(slab_rows):
    longest = lax.axis_size("ctx") * slab_rows // 2
    return -(-longest // slab_rows)


def incoming_state(slab_pair, slab_rows):
    map_now, add_now = slab_pair
    window = window_slabs_of(slab_rows)

    def received(value, distance):
        return shifted(value.astype(jnp.bfloat16), "ctx", distance).astype(jnp.float32)

    def product(left, right):
        return jnp.einsum("hkj,hjl->hkl", left, right, precision=PRECISE_PRODUCT)

    distance = 1
    while 2 * distance < window:
        map_before = received(map_now, distance)
        add_before = received(add_now, distance)
        add_now = product(map_now, add_before) + add_now
        map_now = product(map_now, map_before)
        distance *= 2
    map_last = received(map_now, 1)
    add_last = received(add_now, 1)
    add_far = received(add_now, distance + 1)
    return product(map_last, add_far) + add_last


def latent_attention(
    mla_query, latents, key_up, value_up, positions, docids, doc_starts, head_count
):
    slab_rows = latents.shape[0]
    slabs = lax.axis_size("ctx")
    reach = window_slabs_of(slab_rows)
    window_slabs = min(reach + 1, slabs)
    window_rows = window_slabs * slab_rows
    everything = lax.all_gather(latents, "ctx", tiled=True)
    first_slab = jnp.clip(lax.axis_index("ctx") - reach, 0, slabs - window_slabs)
    key_first = first_slab * slab_rows
    key_rows = lax.dynamic_slice_in_dim(everything, key_first, window_rows, 0)
    latent_part = key_rows[:, :LATENT]
    keys_nope = (
        jnp.dot(latent_part, key_up, preferred_element_type=jnp.float32)
        .astype(jnp.bfloat16)
        .reshape(window_rows, head_count, NOPE)
    )
    values = (
        jnp.dot(latent_part, value_up, preferred_element_type=jnp.float32)
        .astype(jnp.bfloat16)
        .reshape(window_rows, head_count, -1)
    )
    queries = mla_query.reshape(slab_rows, head_count, NOPE + ROPE)
    score_scale = 1.0 / math.sqrt(NOPE + ROPE)
    scores = jnp.einsum(
        "thd,shd->hts", queries[:, :, :NOPE], keys_nope, preferred_element_type=jnp.float32
    )
    scores = (
        scores
        + jnp.einsum(
            "thr,sr->hts",
            queries[:, :, NOPE:],
            key_rows[:, LATENT:],
            preferred_element_type=jnp.float32,
        )
    ) * score_scale
    key_places = key_first + jnp.arange(window_rows, dtype=jnp.int32)
    key_docs = doc_of(key_places, doc_starts)
    allowed = (key_places[None, :] <= positions[:, None]) & (
        key_docs[None, :] == docids[:, None]
    )
    masked = jnp.where(allowed[None], scores, -1e30)
    row_max = jnp.max(masked, axis=2, keepdims=True)
    weights = jnp.where(allowed[None], jnp.exp(masked - row_max), 0.0)
    row_total = jnp.sum(weights, axis=2)
    summed = jnp.einsum(
        "hts,shv->thv", weights.astype(jnp.bfloat16), values, preferred_element_type=jnp.float32
    )
    return (
        (summed / jnp.transpose(row_total)[:, :, None]).astype(jnp.bfloat16).reshape(slab_rows, -1)
    )


def solution(mesh):
    in_specs = (
        P(("batch", "ctx"), None),
        P(("batch", "ctx"), None),
        P(("batch", "ctx"), None),
        P(("batch", "ctx"), None),
        P(("batch", "ctx"), None),
        P(("batch", "ctx"), None),
        P(("batch", "ctx"), None),
        P(),
        P(),
        P("batch"),
    )
    out_specs = (P(("batch", "ctx"), None), P(("batch", "ctx"), None))
    return jax.shard_map(local, mesh=mesh, in_specs=in_specs, out_specs=out_specs, check_vma=False)
```

```python
import math

import jax
import jax.numpy as jnp
from jax import lax
from jax.sharding import PartitionSpec as P

NOPE = 128
ROPE = 64
LATENT = 512
BLOCK = 64


PRECISE_PRODUCT = lax.Precision.HIGHEST


def prefix(array, axis, join, neutral):
    place = lax.axis_index(axis)
    gathered = jax.tree.map(
        lambda a, kind: lax.all_gather(a.astype(kind), axis),
        array,
        jax.tree.map(lambda a: jnp.bfloat16 if a.dtype == jnp.float32 else a.dtype, array),
    )
    state = jax.tree.map(lambda a, e: jnp.zeros_like(a) + jnp.asarray(e, a.dtype), array, neutral)

    def one(step, state):
        return join(
            state,
            jax.tree.map(
                lambda a, own: lax.dynamic_index_in_dim(a, step, 0, False).astype(own.dtype),
                gathered,
                array,
            ),
        )

    return lax.fori_loop(0, place, one, state)


def shifted(block, axis, distance):
    devices = range(lax.axis_size(axis))
    route = [(i - distance, i) for i in devices if i - distance in devices]
    return lax.ppermute(block, axis, route)


def unit_rows(values):
    return values * lax.rsqrt(jnp.sum(values * values, axis=-1, keepdims=True) + 1e-06)


def doc_of(positions, doc_starts):
    match_count = (doc_starts[None, :] <= positions[:, None]).astype(jnp.int32)
    return jnp.sum(match_count, axis=1) - 1


def unit_lower_inverse(strictly_lower):
    length = strictly_lower.shape[-1]
    identity = jnp.eye(length, dtype=jnp.float32)[None]
    result = identity - strictly_lower
    power_term = strictly_lower
    for level_index in range(length.bit_length() - 2):
        power_term = jnp.einsum("hij,hjk->hik", power_term, power_term, precision=PRECISE_PRODUCT)
        result = jnp.einsum(
            "hij,hjk->hik", result, identity + power_term, precision=PRECISE_PRODUCT
        )
    return result


def block_terms(query_unit, keyvec, valvec, logarithm_decay, write_gain, docids, prevdoc):
    length = docids.shape[0]
    cumulative = jnp.cumsum(logarithm_decay, axis=0)
    growth = jnp.exp(cumulative)
    key_plus = keyvec * growth
    key_minus = keyvec * jnp.exp(-cumulative)
    query_plus = query_unit * growth
    places = jnp.arange(length)
    same_doc = docids[:, None] == docids[None, :]
    strict = (places[:, None] > places[None, :]) & same_doc
    causal = (places[:, None] >= places[None, :]) & same_doc
    follow = (docids == prevdoc).astype(jnp.float32)
    inner_prod = jnp.einsum("thk,shk->hts", key_plus, key_minus, precision=PRECISE_PRODUCT)
    strictly_lower = (
        jnp.where(strict[None], inner_prod, 0.0) * jnp.transpose(write_gain)[:, :, None]
    )
    inverse = unit_lower_inverse(strictly_lower)
    value_rhs = jnp.transpose(valvec * write_gain[:, :, None], (1, 0, 2))
    key_rhs = jnp.transpose(key_plus * (write_gain * follow[:, None])[:, :, None], (1, 0, 2))
    value_solution = jnp.einsum("hts,hsv->htv", inverse, value_rhs, precision=PRECISE_PRODUCT)
    solved_key = jnp.einsum("hts,hsk->htk", inverse, key_rhs, precision=PRECISE_PRODUCT)
    mixing = jnp.where(
        causal[None],
        jnp.einsum("thk,shk->hts", query_plus, key_minus, precision=PRECISE_PRODUCT),
        0.0,
    )
    local_output = jnp.einsum("hts,hsv->htv", mixing, value_solution, precision=PRECISE_PRODUCT)
    query_effective = jnp.transpose(query_plus * follow[:, None, None], (1, 0, 2)) - jnp.einsum(
        "hts,hsk->htk", mixing, solved_key, precision=PRECISE_PRODUCT
    )
    last_doc = (docids == docids[length - 1]).astype(jnp.float32)
    key_trailing = (
        keyvec * jnp.exp(cumulative[length - 1][None] - cumulative) * last_doc[:, None, None]
    )
    growth_last = growth[length - 1]
    diagonal_map = growth_last[:, :, None] * jnp.eye(keyvec.shape[2], dtype=jnp.float32)[None]
    handed_operator = follow[length - 1] * diagonal_map - jnp.einsum(
        "shk,hsj->hkj", key_trailing, solved_key, precision=PRECISE_PRODUCT
    )
    handed_update = jnp.einsum(
        "omt,mor->mtr", key_trailing, value_solution, precision=PRECISE_PRODUCT
    )
    return (local_output, query_effective, handed_operator, handed_update)


def compose(prior_slab, successor_slab):
    joined_map = jnp.einsum(
        "hkj,hjl->hkl", successor_slab[0], prior_slab[0], precision=PRECISE_PRODUCT
    )
    combined_increment = (
        jnp.einsum("ytn,yne->yte", successor_slab[0], prior_slab[1], precision=PRECISE_PRODUCT)
        + successor_slab[1]
    )
    return (joined_map, combined_increment)


def local(
    kda_query,
    kda_key,
    kda_value,
    log_decay,
    write_rate,
    mla_query,
    latents,
    key_up,
    value_up,
    doc_lengths,
):
    slab_rows = latents.shape[0]
    head_count = write_rate.shape[1]
    first_row = lax.axis_index("ctx") * slab_rows
    doc_starts = jnp.cumsum(doc_lengths) - doc_lengths
    positions = first_row + jnp.arange(slab_rows, dtype=jnp.int32)
    docids = doc_of(positions, doc_starts)
    query_unit = unit_rows(kda_query.astype(jnp.float32).reshape(slab_rows, head_count, -1))
    keyvec = unit_rows(kda_key.astype(jnp.float32).reshape(slab_rows, head_count, -1))
    valvec = kda_value.astype(jnp.float32).reshape(slab_rows, head_count, -1)
    logarithm_decay = log_decay.astype(jnp.float32).reshape(slab_rows, head_count, -1)
    block_count = slab_rows // BLOCK
    prevdocs = doc_of(first_row + jnp.arange(block_count, dtype=jnp.int32) * BLOCK - 1, doc_starts)

    def shaped(values):
        return values.reshape((block_count, BLOCK) + values.shape[1:])

    block_outs = jax.vmap(block_terms)(
        shaped(query_unit),
        shaped(keyvec),
        shaped(valvec),
        shaped(logarithm_decay),
        shaped(write_rate),
        shaped(docids),
        prevdocs,
    )
    key_dim = keyvec.shape[2]
    value_dim = valvec.shape[2]
    identity_map = jnp.broadcast_to(
        jnp.eye(key_dim, dtype=jnp.float32)[None], (head_count, key_dim, key_dim)
    )
    zero_add = jnp.zeros((head_count, key_dim, value_dim), jnp.float32)

    def advance_block(prefix_pair, block_item):
        map_before, update_from_prior = prefix_pair
        local_output, query_effective, handed_operator, handed_update = block_item
        eff_now = jnp.einsum("htk,hkj->htj", query_effective, map_before, precision=PRECISE_PRODUCT)
        output_current = local_output + jnp.einsum(
            "cor,crm->com", query_effective, update_from_prior, precision=PRECISE_PRODUCT
        )
        map_after = jnp.einsum(
            "hkj,hjl->hkl", handed_operator, map_before, precision=PRECISE_PRODUCT
        )
        increment_later = (
            jnp.einsum(
                "ytn,yne->yte", handed_operator, update_from_prior, precision=PRECISE_PRODUCT
            )
            + handed_update
        )
        return ((map_after, increment_later), (eff_now, output_current))

    slab_pair, per_block = lax.scan(advance_block, (identity_map, zero_add), block_outs)
    effective_everything, output_everything = per_block
    attend_group, group_count = latent_attention(
        mla_query, latents, key_up, value_up, positions, docids, doc_starts, head_count
    )
    carried_in, mla_parts = incoming_state(slab_pair, slab_rows, attend_group, group_count)
    delta_attention_complete = output_everything + jnp.einsum(
        "enzx,nxu->enzu", effective_everything, carried_in, precision=PRECISE_PRODUCT
    )
    kda_out = (
        jnp.transpose(delta_attention_complete, (0, 2, 1, 3))
        .reshape(slab_rows, -1)
        .astype(jnp.bfloat16)
    )
    mla_out = jnp.concatenate(mla_parts, axis=1).reshape(slab_rows, -1)
    return (kda_out, mla_out)


def window_slabs_of(slab_rows):
    longest = lax.axis_size("ctx") * slab_rows // 2
    return -(-longest // slab_rows)


def carry_rounds(slab_rows):
    window = window_slabs_of(slab_rows)
    distance, rounds = 1, 1
    while 2 * distance < window:
        distance, rounds = 2 * distance, rounds + 1
    return rounds


def incoming_state(slab_pair, slab_rows, attend_group, group_count):
    map_now, add_now = slab_pair
    window = window_slabs_of(slab_rows)
    rounds = carry_rounds(slab_rows)
    groups_at = [[] for _ in range(rounds)]
    for group in range(group_count):
        groups_at[group * rounds // group_count].append(group)
    parts = []

    def exchange(values, distances, step):
        sent = tuple(v.astype(jnp.bfloat16) for v in values)
        sent = lax.optimization_barrier(sent)
        got = tuple(shifted(v, "ctx", d) for v, d in zip(sent, distances))
        done = [attend_group(group, sent[0]) for group in groups_at[step]]
        got, done = lax.optimization_barrier((got, done))
        parts.extend(done)
        return tuple(v.astype(jnp.float32) for v in got)

    def product(left, right):
        return jnp.einsum("hkj,hjl->hkl", left, right, precision=PRECISE_PRODUCT)

    distance, step = 1, 0
    while 2 * distance < window:
        map_before, add_before = exchange((map_now, add_now), (distance, distance), step)
        add_now = product(map_now, add_before) + add_now
        map_now = product(map_now, map_before)
        distance, step = 2 * distance, step + 1
    map_last, add_last, add_far = exchange(
        (map_now, add_now, add_now), (1, 1, distance + 1), step
    )
    return product(map_last, add_far) + add_last, parts


def latent_attention(
    mla_query, latents, key_up, value_up, positions, docids, doc_starts, head_count
):
    slab_rows = latents.shape[0]
    slabs = lax.axis_size("ctx")
    reach = window_slabs_of(slab_rows)
    window_slabs = min(reach + 1, slabs)
    window_rows = window_slabs * slab_rows
    everything = lax.all_gather(latents, "ctx", tiled=True)
    first_slab = jnp.clip(lax.axis_index("ctx") - reach, 0, slabs - window_slabs)
    key_first = first_slab * slab_rows
    key_rows = lax.dynamic_slice_in_dim(everything, key_first, window_rows, 0)
    queries = mla_query.reshape(slab_rows, head_count, NOPE + ROPE)
    score_scale = 1.0 / math.sqrt(NOPE + ROPE)
    key_places = key_first + jnp.arange(window_rows, dtype=jnp.int32)
    key_docs = doc_of(key_places, doc_starts)
    allowed = (key_places[None, :] <= positions[:, None]) & (
        key_docs[None, :] == docids[:, None]
    )
    value_width = value_up.shape[1] // head_count
    group_count = carry_rounds(slab_rows)
    while head_count % group_count:
        group_count -= 1
    per_group = head_count // group_count

    def attend_group(group, tie):
        rows, _ = lax.optimization_barrier((key_rows, tie))
        heads = slice(group * per_group, (group + 1) * per_group)
        latent_part = rows[:, :LATENT]
        keys_nope = (
            jnp.dot(
                latent_part,
                key_up[:, group * per_group * NOPE : (group + 1) * per_group * NOPE],
                preferred_element_type=jnp.float32,
            )
            .astype(jnp.bfloat16)
            .reshape(window_rows, per_group, NOPE)
        )
        values = (
            jnp.dot(
                latent_part,
                value_up[
                    :, group * per_group * value_width : (group + 1) * per_group * value_width
                ],
                preferred_element_type=jnp.float32,
            )
            .astype(jnp.bfloat16)
            .reshape(window_rows, per_group, value_width)
        )
        scores = jnp.einsum(
            "thd,shd->hts",
            queries[:, heads, :NOPE],
            keys_nope,
            preferred_element_type=jnp.float32,
        )
        scores = (
            scores
            + jnp.einsum(
                "thr,sr->hts",
                queries[:, heads, NOPE:],
                rows[:, LATENT:],
                preferred_element_type=jnp.float32,
            )
        ) * score_scale
        masked = jnp.where(allowed[None], scores, -1e30)
        row_max = jnp.max(masked, axis=2, keepdims=True)
        weights = jnp.where(allowed[None], jnp.exp(masked - row_max), 0.0)
        row_total = jnp.sum(weights, axis=2)
        summed = jnp.einsum(
            "hts,shv->thv",
            weights.astype(jnp.bfloat16),
            values,
            preferred_element_type=jnp.float32,
        )
        return (summed / jnp.transpose(row_total)[:, :, None]).astype(jnp.bfloat16)

    return attend_group, group_count


def solution(mesh):
    in_specs = (
        P(("batch", "ctx"), None),
        P(("batch", "ctx"), None),
        P(("batch", "ctx"), None),
        P(("batch", "ctx"), None),
        P(("batch", "ctx"), None),
        P(("batch", "ctx"), None),
        P(("batch", "ctx"), None),
        P(),
        P(),
        P("batch"),
    )
    out_specs = (P(("batch", "ctx"), None), P(("batch", "ctx"), None))
    return jax.shard_map(local, mesh=mesh, in_specs=in_specs, out_specs=out_specs, check_vma=False)
```

```python
import math

import jax
import jax.numpy as jnp
from jax import lax
from jax.sharding import PartitionSpec as P

NOPE = 128
ROPE = 64
LATENT = 512
BLOCK = 64


PRECISE_PRODUCT = lax.Precision.HIGHEST


def prefix(array, axis, join, neutral):
    place = lax.axis_index(axis)
    gathered = jax.tree.map(
        lambda a, kind: lax.all_gather(a.astype(kind), axis),
        array,
        jax.tree.map(lambda a: jnp.bfloat16 if a.dtype == jnp.float32 else a.dtype, array),
    )
    state = jax.tree.map(lambda a, e: jnp.zeros_like(a) + jnp.asarray(e, a.dtype), array, neutral)

    def one(step, state):
        return join(
            state,
            jax.tree.map(
                lambda a, own: lax.dynamic_index_in_dim(a, step, 0, False).astype(own.dtype),
                gathered,
                array,
            ),
        )

    return lax.fori_loop(0, place, one, state)


def shifted(block, axis, distance):
    devices = range(lax.axis_size(axis))
    route = [(i - distance, i) for i in devices if i - distance in devices]
    return lax.ppermute(block, axis, route)


def unit_rows(values):
    return values * lax.rsqrt(jnp.sum(values * values, axis=-1, keepdims=True) + 1e-06)


def doc_of(positions, doc_starts):
    match_count = (doc_starts[None, :] <= positions[:, None]).astype(jnp.int32)
    return jnp.sum(match_count, axis=1) - 1


def unit_lower_inverse(strictly_lower):
    length = strictly_lower.shape[-1]
    identity = jnp.eye(length, dtype=jnp.float32)[None]
    result = identity - strictly_lower
    power_term = strictly_lower
    for level_index in range(length.bit_length() - 2):
        power_term = jnp.einsum("hij,hjk->hik", power_term, power_term, precision=PRECISE_PRODUCT)
        result = jnp.einsum(
            "hij,hjk->hik", result, identity + power_term, precision=PRECISE_PRODUCT
        )
    return result


def block_terms(query_unit, keyvec, valvec, logarithm_decay, write_gain, docids, prevdoc):
    length = docids.shape[0]
    cumulative = jnp.cumsum(logarithm_decay, axis=0)
    growth = jnp.exp(cumulative)
    key_plus = keyvec * growth
    key_minus = keyvec * jnp.exp(-cumulative)
    query_plus = query_unit * growth
    places = jnp.arange(length)
    same_doc = docids[:, None] == docids[None, :]
    strict = (places[:, None] > places[None, :]) & same_doc
    causal = (places[:, None] >= places[None, :]) & same_doc
    follow = (docids == prevdoc).astype(jnp.float32)
    inner_prod = jnp.einsum("thk,shk->hts", key_plus, key_minus, precision=PRECISE_PRODUCT)
    strictly_lower = (
        jnp.where(strict[None], inner_prod, 0.0) * jnp.transpose(write_gain)[:, :, None]
    )
    inverse = unit_lower_inverse(strictly_lower)
    value_rhs = jnp.transpose(valvec * write_gain[:, :, None], (1, 0, 2))
    key_rhs = jnp.transpose(key_plus * (write_gain * follow[:, None])[:, :, None], (1, 0, 2))
    value_solution = jnp.einsum("hts,hsv->htv", inverse, value_rhs, precision=PRECISE_PRODUCT)
    solved_key = jnp.einsum("hts,hsk->htk", inverse, key_rhs, precision=PRECISE_PRODUCT)
    mixing = jnp.where(
        causal[None],
        jnp.einsum("thk,shk->hts", query_plus, key_minus, precision=PRECISE_PRODUCT),
        0.0,
    )
    local_output = jnp.einsum("hts,hsv->htv", mixing, value_solution, precision=PRECISE_PRODUCT)
    query_effective = jnp.transpose(query_plus * follow[:, None, None], (1, 0, 2)) - jnp.einsum(
        "hts,hsk->htk", mixing, solved_key, precision=PRECISE_PRODUCT
    )
    last_doc = (docids == docids[length - 1]).astype(jnp.float32)
    key_trailing = (
        keyvec * jnp.exp(cumulative[length - 1][None] - cumulative) * last_doc[:, None, None]
    )
    growth_last = growth[length - 1]
    diagonal_map = growth_last[:, :, None] * jnp.eye(keyvec.shape[2], dtype=jnp.float32)[None]
    handed_operator = follow[length - 1] * diagonal_map - jnp.einsum(
        "shk,hsj->hkj", key_trailing, solved_key, precision=PRECISE_PRODUCT
    )
    handed_update = jnp.einsum(
        "omt,mor->mtr", key_trailing, value_solution, precision=PRECISE_PRODUCT
    )
    return (local_output, query_effective, handed_operator, handed_update)


def compose(prior_slab, successor_slab):
    joined_map = jnp.einsum(
        "hkj,hjl->hkl", successor_slab[0], prior_slab[0], precision=PRECISE_PRODUCT
    )
    combined_increment = (
        jnp.einsum("ytn,yne->yte", successor_slab[0], prior_slab[1], precision=PRECISE_PRODUCT)
        + successor_slab[1]
    )
    return (joined_map, combined_increment)


def local(
    kda_query,
    kda_key,
    kda_value,
    log_decay,
    write_rate,
    mla_query,
    latents,
    key_up,
    value_up,
    doc_lengths,
):
    slab_rows = latents.shape[0]
    head_count = write_rate.shape[1]
    first_row = lax.axis_index("ctx") * slab_rows
    doc_starts = jnp.cumsum(doc_lengths) - doc_lengths
    positions = first_row + jnp.arange(slab_rows, dtype=jnp.int32)
    docids = doc_of(positions, doc_starts)
    query_unit = unit_rows(kda_query.astype(jnp.float32).reshape(slab_rows, head_count, -1))
    keyvec = unit_rows(kda_key.astype(jnp.float32).reshape(slab_rows, head_count, -1))
    valvec = kda_value.astype(jnp.float32).reshape(slab_rows, head_count, -1)
    logarithm_decay = log_decay.astype(jnp.float32).reshape(slab_rows, head_count, -1)
    block_count = slab_rows // BLOCK
    prevdocs = doc_of(first_row + jnp.arange(block_count, dtype=jnp.int32) * BLOCK - 1, doc_starts)

    def shaped(values):
        return values.reshape((block_count, BLOCK) + values.shape[1:])

    block_outs = jax.vmap(block_terms)(
        shaped(query_unit),
        shaped(keyvec),
        shaped(valvec),
        shaped(logarithm_decay),
        shaped(write_rate),
        shaped(docids),
        prevdocs,
    )
    key_dim = keyvec.shape[2]
    value_dim = valvec.shape[2]
    identity_map = jnp.broadcast_to(
        jnp.eye(key_dim, dtype=jnp.float32)[None], (head_count, key_dim, key_dim)
    )
    zero_add = jnp.zeros((head_count, key_dim, value_dim), jnp.float32)

    def advance_block(prefix_pair, block_item):
        map_before, update_from_prior = prefix_pair
        local_output, query_effective, handed_operator, handed_update = block_item
        eff_now = jnp.einsum("htk,hkj->htj", query_effective, map_before, precision=PRECISE_PRODUCT)
        output_current = local_output + jnp.einsum(
            "cor,crm->com", query_effective, update_from_prior, precision=PRECISE_PRODUCT
        )
        map_after = jnp.einsum(
            "hkj,hjl->hkl", handed_operator, map_before, precision=PRECISE_PRODUCT
        )
        increment_later = (
            jnp.einsum(
                "ytn,yne->yte", handed_operator, update_from_prior, precision=PRECISE_PRODUCT
            )
            + handed_update
        )
        return ((map_after, increment_later), (eff_now, output_current))

    local_output, query_effective, handed_operator, handed_update = block_outs
    slab_pair = (handed_operator[0], handed_update[0])
    effective_blocks, output_blocks = [query_effective[0]], [local_output[0]]
    for block in range(1, block_count):
        slab_pair, (eff_now, output_current) = advance_block(
            slab_pair,
            (local_output[block], query_effective[block], handed_operator[block], handed_update[block]),
        )
        effective_blocks.append(eff_now)
        output_blocks.append(output_current)
    effective_everything = jnp.stack(effective_blocks)
    output_everything = jnp.stack(output_blocks)
    attend_group, group_count = latent_attention(
        mla_query, latents, key_up, value_up, positions, docids, doc_starts, head_count
    )
    carried_in, mla_parts = incoming_state(slab_pair, slab_rows, attend_group, group_count)
    delta_attention_complete = output_everything + jnp.einsum(
        "enzx,nxu->enzu", effective_everything, carried_in, precision=PRECISE_PRODUCT
    )
    kda_out = (
        jnp.transpose(delta_attention_complete, (0, 2, 1, 3))
        .reshape(slab_rows, -1)
        .astype(jnp.bfloat16)
    )
    mla_out = jnp.concatenate(mla_parts, axis=1).reshape(slab_rows, -1)
    return (kda_out, mla_out)


def window_slabs_of(slab_rows):
    longest = lax.axis_size("ctx") * slab_rows // 2
    return -(-longest // slab_rows)


def carry_rounds(slab_rows):
    window = window_slabs_of(slab_rows)
    distance, rounds = 1, 1
    while 2 * distance < window:
        distance, rounds = 2 * distance, rounds + 1
    return rounds


def incoming_state(slab_pair, slab_rows, attend_group, group_count):
    map_now, add_now = slab_pair
    window = window_slabs_of(slab_rows)
    rounds = carry_rounds(slab_rows)
    groups_at = [[] for _ in range(rounds)]
    for group in range(group_count):
        groups_at[group * rounds // group_count].append(group)
    parts = []

    def exchange(values, distances, step):
        sent = tuple(v.astype(jnp.bfloat16) for v in values)
        sent = lax.optimization_barrier(sent)
        got = tuple(shifted(v, "ctx", d) for v, d in zip(sent, distances))
        done = [attend_group(group, sent[0]) for group in groups_at[step]]
        got, done = lax.optimization_barrier((got, done))
        parts.extend(done)
        return tuple(v.astype(jnp.float32) for v in got)

    def product(left, right):
        return jnp.einsum("hkj,hjl->hkl", left, right, precision=PRECISE_PRODUCT)

    value_dim = add_now.shape[2]
    distance, step = 1, 0
    while 2 * distance < window:
        (before,) = exchange((jnp.concatenate([add_now, map_now], axis=2),), (distance,), step)
        joined = product(map_now, before)
        add_now = joined[:, :, :value_dim] + add_now
        map_now = joined[:, :, value_dim:]
        distance, step = 2 * distance, step + 1
    last, add_far = exchange(
        (jnp.concatenate([add_now, map_now], axis=2), add_now), (1, distance + 1), step
    )
    return product(last[:, :, value_dim:], add_far) + last[:, :, :value_dim], parts


def latent_attention(
    mla_query, latents, key_up, value_up, positions, docids, doc_starts, head_count
):
    slab_rows = latents.shape[0]
    slabs = lax.axis_size("ctx")
    reach = window_slabs_of(slab_rows)
    window_slabs = min(reach + 1, slabs)
    window_rows = window_slabs * slab_rows
    everything = lax.all_gather(latents, "ctx", tiled=True)
    first_slab = jnp.clip(lax.axis_index("ctx") - reach, 0, slabs - window_slabs)
    key_first = first_slab * slab_rows
    key_rows = lax.dynamic_slice_in_dim(everything, key_first, window_rows, 0)
    queries = mla_query.reshape(slab_rows, head_count, NOPE + ROPE)
    score_scale = 1.0 / math.sqrt(NOPE + ROPE)
    key_places = key_first + jnp.arange(window_rows, dtype=jnp.int32)
    key_docs = doc_of(key_places, doc_starts)
    allowed = (key_places[None, :] <= positions[:, None]) & (
        key_docs[None, :] == docids[:, None]
    )
    value_width = value_up.shape[1] // head_count
    group_count = carry_rounds(slab_rows)
    while head_count % group_count:
        group_count -= 1
    per_group = head_count // group_count

    def attend_group(group, tie):
        rows, _ = lax.optimization_barrier((key_rows, tie))
        heads = slice(group * per_group, (group + 1) * per_group)
        latent_part = rows[:, :LATENT]
        keys_nope = (
            jnp.dot(
                latent_part,
                key_up[:, group * per_group * NOPE : (group + 1) * per_group * NOPE],
                preferred_element_type=jnp.float32,
            )
            .astype(jnp.bfloat16)
            .reshape(window_rows, per_group, NOPE)
        )
        values = (
            jnp.dot(
                latent_part,
                value_up[
                    :, group * per_group * value_width : (group + 1) * per_group * value_width
                ],
                preferred_element_type=jnp.float32,
            )
            .astype(jnp.bfloat16)
            .reshape(window_rows, per_group, value_width)
        )
        scores = jnp.einsum(
            "thd,shd->hts",
            queries[:, heads, :NOPE],
            keys_nope,
            preferred_element_type=jnp.float32,
        )
        scores = (
            scores
            + jnp.einsum(
                "thr,sr->hts",
                queries[:, heads, NOPE:],
                rows[:, LATENT:],
                preferred_element_type=jnp.float32,
            )
        ) * score_scale
        masked = jnp.where(allowed[None], scores, -1e30)
        row_max = jnp.max(masked, axis=2, keepdims=True)
        weights = jnp.where(allowed[None], jnp.exp(masked - row_max), 0.0)
        row_total = jnp.sum(weights, axis=2)
        summed = jnp.einsum(
            "hts,shv->thv",
            weights.astype(jnp.bfloat16),
            values,
            preferred_element_type=jnp.float32,
        )
        return (summed / jnp.transpose(row_total)[:, :, None]).astype(jnp.bfloat16)

    return attend_group, group_count


def solution(mesh):
    in_specs = (
        P(("batch", "ctx"), None),
        P(("batch", "ctx"), None),
        P(("batch", "ctx"), None),
        P(("batch", "ctx"), None),
        P(("batch", "ctx"), None),
        P(("batch", "ctx"), None),
        P(("batch", "ctx"), None),
        P(),
        P(),
        P("batch"),
    )
    out_specs = (P(("batch", "ctx"), None), P(("batch", "ctx"), None))
    return jax.shard_map(local, mesh=mesh, in_specs=in_specs, out_specs=out_specs, check_vma=False)
```

```python
import math

import jax
import jax.numpy as jnp
from jax import lax
from jax.sharding import PartitionSpec as P

NOPE = 128
ROPE = 64
LATENT = 512
BLOCK = 64


PRECISE_PRODUCT = lax.Precision.HIGHEST


def prefix(array, axis, join, neutral):
    place = lax.axis_index(axis)
    gathered = jax.tree.map(
        lambda a, kind: lax.all_gather(a.astype(kind), axis),
        array,
        jax.tree.map(lambda a: jnp.bfloat16 if a.dtype == jnp.float32 else a.dtype, array),
    )
    state = jax.tree.map(lambda a, e: jnp.zeros_like(a) + jnp.asarray(e, a.dtype), array, neutral)

    def one(step, state):
        return join(
            state,
            jax.tree.map(
                lambda a, own: lax.dynamic_index_in_dim(a, step, 0, False).astype(own.dtype),
                gathered,
                array,
            ),
        )

    return lax.fori_loop(0, place, one, state)


def shifted(block, axis, distance):
    devices = range(lax.axis_size(axis))
    route = [(i - distance, i) for i in devices if i - distance in devices]
    return lax.ppermute(block, axis, route)


def unit_rows(values):
    return values * lax.rsqrt(jnp.sum(values * values, axis=-1, keepdims=True) + 1e-06)


def doc_of(positions, doc_starts):
    match_count = (doc_starts[None, :] <= positions[:, None]).astype(jnp.int32)
    return jnp.sum(match_count, axis=1) - 1


def unit_lower_inverse(strictly_lower):
    length = strictly_lower.shape[-1]
    identity = jnp.eye(length, dtype=jnp.float32)[None]
    result = identity - strictly_lower
    power_term = strictly_lower
    for level_index in range(length.bit_length() - 2):
        power_term = jnp.einsum("hij,hjk->hik", power_term, power_term, precision=PRECISE_PRODUCT)
        result = jnp.einsum(
            "hij,hjk->hik", result, identity + power_term, precision=PRECISE_PRODUCT
        )
    return result


def block_terms(query_unit, keyvec, valvec, logarithm_decay, write_gain, docids, prevdoc):
    length = docids.shape[0]
    cumulative = jnp.cumsum(logarithm_decay, axis=0)
    growth = jnp.exp(cumulative)
    key_plus = keyvec * growth
    key_minus = keyvec * jnp.exp(-cumulative)
    query_plus = query_unit * growth
    places = jnp.arange(length)
    same_doc = docids[:, None] == docids[None, :]
    strict = (places[:, None] > places[None, :]) & same_doc
    causal = (places[:, None] >= places[None, :]) & same_doc
    follow = (docids == prevdoc).astype(jnp.float32)
    inner_prod = jnp.einsum("thk,shk->hts", key_plus, key_minus, precision=PRECISE_PRODUCT)
    strictly_lower = (
        jnp.where(strict[None], inner_prod, 0.0) * jnp.transpose(write_gain)[:, :, None]
    )
    inverse = unit_lower_inverse(strictly_lower)
    value_rhs = jnp.transpose(valvec * write_gain[:, :, None], (1, 0, 2))
    key_rhs = jnp.transpose(key_plus * (write_gain * follow[:, None])[:, :, None], (1, 0, 2))
    value_solution = jnp.einsum("hts,hsv->htv", inverse, value_rhs, precision=PRECISE_PRODUCT)
    solved_key = jnp.einsum("hts,hsk->htk", inverse, key_rhs, precision=PRECISE_PRODUCT)
    mixing = jnp.where(
        causal[None],
        jnp.einsum("thk,shk->hts", query_plus, key_minus, precision=PRECISE_PRODUCT),
        0.0,
    )
    local_output = jnp.einsum("hts,hsv->htv", mixing, value_solution, precision=PRECISE_PRODUCT)
    query_effective = jnp.transpose(query_plus * follow[:, None, None], (1, 0, 2)) - jnp.einsum(
        "hts,hsk->htk", mixing, solved_key, precision=PRECISE_PRODUCT
    )
    last_doc = (docids == docids[length - 1]).astype(jnp.float32)
    key_trailing = (
        keyvec * jnp.exp(cumulative[length - 1][None] - cumulative) * last_doc[:, None, None]
    )
    growth_last = growth[length - 1]
    diagonal_map = growth_last[:, :, None] * jnp.eye(keyvec.shape[2], dtype=jnp.float32)[None]
    handed_operator = follow[length - 1] * diagonal_map - jnp.einsum(
        "shk,hsj->hkj", key_trailing, solved_key, precision=PRECISE_PRODUCT
    )
    handed_update = jnp.einsum(
        "omt,mor->mtr", key_trailing, value_solution, precision=PRECISE_PRODUCT
    )
    return (local_output, query_effective, handed_operator, handed_update)


def compose(prior_slab, successor_slab):
    joined_map = jnp.einsum(
        "hkj,hjl->hkl", successor_slab[0], prior_slab[0], precision=PRECISE_PRODUCT
    )
    combined_increment = (
        jnp.einsum("ytn,yne->yte", successor_slab[0], prior_slab[1], precision=PRECISE_PRODUCT)
        + successor_slab[1]
    )
    return (joined_map, combined_increment)


def local(
    kda_query,
    kda_key,
    kda_value,
    log_decay,
    write_rate,
    mla_query,
    latents,
    key_up,
    value_up,
    doc_lengths,
):
    slab_rows = latents.shape[0]
    head_count = write_rate.shape[1]
    first_row = lax.axis_index("ctx") * slab_rows
    doc_starts = jnp.cumsum(doc_lengths) - doc_lengths
    positions = first_row + jnp.arange(slab_rows, dtype=jnp.int32)
    docids = doc_of(positions, doc_starts)
    query_unit = unit_rows(kda_query.astype(jnp.float32).reshape(slab_rows, head_count, -1))
    keyvec = unit_rows(kda_key.astype(jnp.float32).reshape(slab_rows, head_count, -1))
    valvec = kda_value.astype(jnp.float32).reshape(slab_rows, head_count, -1)
    logarithm_decay = log_decay.astype(jnp.float32).reshape(slab_rows, head_count, -1)
    block_count = slab_rows // BLOCK
    prevdocs = doc_of(first_row + jnp.arange(block_count, dtype=jnp.int32) * BLOCK - 1, doc_starts)

    def shaped(values):
        return values.reshape((block_count, BLOCK) + values.shape[1:])

    block_outs = jax.vmap(block_terms)(
        shaped(query_unit),
        shaped(keyvec),
        shaped(valvec),
        shaped(logarithm_decay),
        shaped(write_rate),
        shaped(docids),
        prevdocs,
    )
    key_dim = keyvec.shape[2]
    value_dim = valvec.shape[2]
    identity_map = jnp.broadcast_to(
        jnp.eye(key_dim, dtype=jnp.float32)[None], (head_count, key_dim, key_dim)
    )
    zero_add = jnp.zeros((head_count, key_dim, value_dim), jnp.float32)

    def advance_block(prefix_pair, block_item):
        map_before, update_from_prior = prefix_pair
        local_output, query_effective, handed_operator, handed_update = block_item
        eff_now = jnp.einsum("htk,hkj->htj", query_effective, map_before, precision=PRECISE_PRODUCT)
        output_current = local_output + jnp.einsum(
            "cor,crm->com", query_effective, update_from_prior, precision=PRECISE_PRODUCT
        )
        map_after = jnp.einsum(
            "hkj,hjl->hkl", handed_operator, map_before, precision=PRECISE_PRODUCT
        )
        increment_later = (
            jnp.einsum(
                "ytn,yne->yte", handed_operator, update_from_prior, precision=PRECISE_PRODUCT
            )
            + handed_update
        )
        return ((map_after, increment_later), (eff_now, output_current))

    local_output, query_effective, handed_operator, handed_update = block_outs
    slab_pair = (handed_operator[0], handed_update[0])
    effective_blocks, output_blocks = [query_effective[0]], [local_output[0]]
    for block in range(1, block_count):
        slab_pair, (eff_now, output_current) = advance_block(
            slab_pair,
            (local_output[block], query_effective[block], handed_operator[block], handed_update[block]),
        )
        effective_blocks.append(eff_now)
        output_blocks.append(output_current)
    effective_everything = jnp.stack(effective_blocks)
    output_everything = jnp.stack(output_blocks)
    attend_group, group_count = latent_attention(
        mla_query, latents, key_up, value_up, positions, docids, doc_starts, head_count
    )
    carried_in, mla_parts = incoming_state(slab_pair, slab_rows, attend_group, group_count)
    delta_attention_complete = output_everything + jnp.einsum(
        "enzx,nxu->enzu", effective_everything, carried_in, precision=PRECISE_PRODUCT
    )
    kda_out = (
        jnp.transpose(delta_attention_complete, (0, 2, 1, 3))
        .reshape(slab_rows, -1)
        .astype(jnp.bfloat16)
    )
    mla_out = jnp.concatenate(mla_parts, axis=1).reshape(slab_rows, -1)
    return (kda_out, mla_out)


def window_slabs_of(slab_rows):
    longest = lax.axis_size("ctx") * slab_rows // 2
    return -(-longest // slab_rows)


def carry_rounds(slab_rows):
    window = window_slabs_of(slab_rows)
    distance, rounds = 1, 2
    while 2 * distance < window:
        distance, rounds = 2 * distance, rounds + 1
    return rounds


def incoming_state(slab_pair, slab_rows, attend_group, group_count):
    map_now, add_now = slab_pair
    window = window_slabs_of(slab_rows)
    rounds = carry_rounds(slab_rows)
    groups_at = [[] for _ in range(rounds)]
    for group in range(group_count):
        groups_at[rounds - group_count + group if rounds > group_count else group * rounds // group_count].append(group)
    parts = []

    def exchange(value, distance, step):
        sent = lax.optimization_barrier(value.astype(jnp.bfloat16))
        got = shifted(sent, "ctx", distance)
        done = [attend_group(group, sent) for group in groups_at[step]]
        got, done = lax.optimization_barrier((got, done))
        parts.extend(done)
        return got.astype(jnp.float32)

    def product(left, right):
        return jnp.einsum("hkj,hjl->hkl", left, right, precision=PRECISE_PRODUCT)

    value_dim = add_now.shape[2]
    distance, step = 1, 0
    while 2 * distance < window:
        before = exchange(jnp.concatenate([add_now, map_now], axis=2), distance, step)
        joined = product(map_now, before)
        add_now = joined[:, :, :value_dim] + add_now
        map_now = joined[:, :, value_dim:]
        distance, step = 2 * distance, step + 1
    add_now = product(map_now, exchange(add_now, distance, step)) + add_now
    return exchange(add_now, 1, step + 1), parts


def latent_attention(
    mla_query, latents, key_up, value_up, positions, docids, doc_starts, head_count
):
    slab_rows = latents.shape[0]
    slabs = lax.axis_size("ctx")
    reach = window_slabs_of(slab_rows)
    window_slabs = min(reach + 1, slabs)
    window_rows = window_slabs * slab_rows
    everything = lax.all_gather(latents, "ctx", tiled=True)
    first_slab = jnp.clip(lax.axis_index("ctx") - reach, 0, slabs - window_slabs)
    key_first = first_slab * slab_rows
    key_rows = lax.dynamic_slice_in_dim(everything, key_first, window_rows, 0)
    queries = mla_query.reshape(slab_rows, head_count, NOPE + ROPE)
    score_scale = 1.0 / math.sqrt(NOPE + ROPE)
    key_places = key_first + jnp.arange(window_rows, dtype=jnp.int32)
    key_docs = doc_of(key_places, doc_starts)
    allowed = (key_places[None, :] <= positions[:, None]) & (
        key_docs[None, :] == docids[:, None]
    )
    value_width = value_up.shape[1] // head_count
    group_count = carry_rounds(slab_rows)
    while head_count % group_count:
        group_count -= 1
    per_group = head_count // group_count

    def attend_group(group, tie):
        rows, _ = lax.optimization_barrier((key_rows, tie))
        heads = slice(group * per_group, (group + 1) * per_group)
        latent_part = rows[:, :LATENT]
        keys_nope = (
            jnp.dot(
                latent_part,
                key_up[:, group * per_group * NOPE : (group + 1) * per_group * NOPE],
                preferred_element_type=jnp.float32,
            )
            .astype(jnp.bfloat16)
            .reshape(window_rows, per_group, NOPE)
        )
        values = (
            jnp.dot(
                latent_part,
                value_up[
                    :, group * per_group * value_width : (group + 1) * per_group * value_width
                ],
                preferred_element_type=jnp.float32,
            )
            .astype(jnp.bfloat16)
            .reshape(window_rows, per_group, value_width)
        )
        scores = jnp.einsum(
            "thd,shd->hts",
            queries[:, heads, :NOPE],
            keys_nope,
            preferred_element_type=jnp.float32,
        )
        scores = (
            scores
            + jnp.einsum(
                "thr,sr->hts",
                queries[:, heads, NOPE:],
                rows[:, LATENT:],
                preferred_element_type=jnp.float32,
            )
        ) * score_scale
        masked = jnp.where(allowed[None], scores, -1e30)
        row_max = jnp.max(masked, axis=2, keepdims=True)
        weights = jnp.where(allowed[None], jnp.exp(masked - row_max), 0.0)
        row_total = jnp.sum(weights, axis=2)
        summed = jnp.einsum(
            "hts,shv->thv",
            weights.astype(jnp.bfloat16),
            values,
            preferred_element_type=jnp.float32,
        )
        return (summed / jnp.transpose(row_total)[:, :, None]).astype(jnp.bfloat16)

    return attend_group, group_count


def solution(mesh):
    in_specs = (
        P(("batch", "ctx"), None),
        P(("batch", "ctx"), None),
        P(("batch", "ctx"), None),
        P(("batch", "ctx"), None),
        P(("batch", "ctx"), None),
        P(("batch", "ctx"), None),
        P(("batch", "ctx"), None),
        P(),
        P(),
        P("batch"),
    )
    out_specs = (P(("batch", "ctx"), None), P(("batch", "ctx"), None))
    return jax.shard_map(local, mesh=mesh, in_specs=in_specs, out_specs=out_specs, check_vma=False)
```

```python
import math

import jax
import jax.numpy as jnp
from jax import lax
from jax.sharding import PartitionSpec as P

NOPE = 128
ROPE = 64
LATENT = 512
BLOCK = 64


PRECISE_PRODUCT = lax.Precision.HIGHEST


def prefix(array, axis, join, neutral):
    place = lax.axis_index(axis)
    gathered = jax.tree.map(
        lambda a, kind: lax.all_gather(a.astype(kind), axis),
        array,
        jax.tree.map(lambda a: jnp.bfloat16 if a.dtype == jnp.float32 else a.dtype, array),
    )
    state = jax.tree.map(lambda a, e: jnp.zeros_like(a) + jnp.asarray(e, a.dtype), array, neutral)

    def one(step, state):
        return join(
            state,
            jax.tree.map(
                lambda a, own: lax.dynamic_index_in_dim(a, step, 0, False).astype(own.dtype),
                gathered,
                array,
            ),
        )

    return lax.fori_loop(0, place, one, state)


def shifted(block, axis, distance):
    devices = range(lax.axis_size(axis))
    route = [(i - distance, i) for i in devices if i - distance in devices]
    return lax.ppermute(block, axis, route)


def unit_rows(values):
    return values * lax.rsqrt(jnp.sum(values * values, axis=-1, keepdims=True) + 1e-06)


def doc_of(positions, doc_starts):
    match_count = (doc_starts[None, :] <= positions[:, None]).astype(jnp.int32)
    return jnp.sum(match_count, axis=1) - 1


def unit_lower_inverse(strictly_lower):
    length = strictly_lower.shape[-1]
    identity = jnp.eye(length, dtype=jnp.float32)[None]
    result = identity - strictly_lower
    power_term = strictly_lower
    for level_index in range(length.bit_length() - 2):
        power_term = jnp.einsum("hij,hjk->hik", power_term, power_term, precision=PRECISE_PRODUCT)
        result = jnp.einsum(
            "hij,hjk->hik", result, identity + power_term, precision=PRECISE_PRODUCT
        )
    return result


def block_terms(query_unit, keyvec, valvec, logarithm_decay, write_gain, docids, prevdoc):
    length = docids.shape[0]
    cumulative = jnp.cumsum(logarithm_decay, axis=0)
    growth = jnp.exp(cumulative)
    key_plus = keyvec * growth
    key_minus = keyvec * jnp.exp(-cumulative)
    query_plus = query_unit * growth
    places = jnp.arange(length)
    same_doc = docids[:, None] == docids[None, :]
    strict = (places[:, None] > places[None, :]) & same_doc
    causal = (places[:, None] >= places[None, :]) & same_doc
    follow = (docids == prevdoc).astype(jnp.float32)
    inner_prod = jnp.einsum("thk,shk->hts", key_plus, key_minus, precision=PRECISE_PRODUCT)
    strictly_lower = (
        jnp.where(strict[None], inner_prod, 0.0) * jnp.transpose(write_gain)[:, :, None]
    )
    inverse = unit_lower_inverse(strictly_lower)
    value_rhs = jnp.transpose(valvec * write_gain[:, :, None], (1, 0, 2))
    key_rhs = jnp.transpose(key_plus * (write_gain * follow[:, None])[:, :, None], (1, 0, 2))
    value_solution = jnp.einsum("hts,hsv->htv", inverse, value_rhs, precision=PRECISE_PRODUCT)
    solved_key = jnp.einsum("hts,hsk->htk", inverse, key_rhs, precision=PRECISE_PRODUCT)
    mixing = jnp.where(
        causal[None],
        jnp.einsum("thk,shk->hts", query_plus, key_minus, precision=PRECISE_PRODUCT),
        0.0,
    )
    local_output = jnp.einsum("hts,hsv->htv", mixing, value_solution, precision=PRECISE_PRODUCT)
    query_effective = jnp.transpose(query_plus * follow[:, None, None], (1, 0, 2)) - jnp.einsum(
        "hts,hsk->htk", mixing, solved_key, precision=PRECISE_PRODUCT
    )
    last_doc = (docids == docids[length - 1]).astype(jnp.float32)
    key_trailing = (
        keyvec * jnp.exp(cumulative[length - 1][None] - cumulative) * last_doc[:, None, None]
    )
    growth_last = growth[length - 1]
    diagonal_map = growth_last[:, :, None] * jnp.eye(keyvec.shape[2], dtype=jnp.float32)[None]
    handed_operator = follow[length - 1] * diagonal_map - jnp.einsum(
        "shk,hsj->hkj", key_trailing, solved_key, precision=PRECISE_PRODUCT
    )
    handed_update = jnp.einsum(
        "omt,mor->mtr", key_trailing, value_solution, precision=PRECISE_PRODUCT
    )
    return (local_output, query_effective, handed_operator, handed_update)


def compose(prior_slab, successor_slab):
    joined_map = jnp.einsum(
        "hkj,hjl->hkl", successor_slab[0], prior_slab[0], precision=PRECISE_PRODUCT
    )
    combined_increment = (
        jnp.einsum("ytn,yne->yte", successor_slab[0], prior_slab[1], precision=PRECISE_PRODUCT)
        + successor_slab[1]
    )
    return (joined_map, combined_increment)


def local(
    kda_query,
    kda_key,
    kda_value,
    log_decay,
    write_rate,
    mla_query,
    latents,
    key_up,
    value_up,
    doc_lengths,
):
    slab_rows = latents.shape[0]
    head_count = write_rate.shape[1]
    first_row = lax.axis_index("ctx") * slab_rows
    doc_starts = jnp.cumsum(doc_lengths) - doc_lengths
    positions = first_row + jnp.arange(slab_rows, dtype=jnp.int32)
    docids = doc_of(positions, doc_starts)
    query_unit = unit_rows(kda_query.astype(jnp.float32).reshape(slab_rows, head_count, -1))
    keyvec = unit_rows(kda_key.astype(jnp.float32).reshape(slab_rows, head_count, -1))
    valvec = kda_value.astype(jnp.float32).reshape(slab_rows, head_count, -1)
    logarithm_decay = log_decay.astype(jnp.float32).reshape(slab_rows, head_count, -1)
    held, held_after = latents[None], []

    def next_latents(held, stage):
        if len(held_after) < len(latent_rounds(slab_rows)):
            held = latent_round(held, slab_rows, len(held_after))
            held, stage = lax.optimization_barrier((held, stage))
            held_after.append(held.shape[0])
        return held, stage

    held, (query_unit, keyvec, valvec, logarithm_decay) = next_latents(
        held, (query_unit, keyvec, valvec, logarithm_decay)
    )
    block_count = slab_rows // BLOCK
    prevdocs = doc_of(first_row + jnp.arange(block_count, dtype=jnp.int32) * BLOCK - 1, doc_starts)

    def shaped(values):
        return values.reshape((block_count, BLOCK) + values.shape[1:])

    block_outs = jax.vmap(block_terms)(
        shaped(query_unit),
        shaped(keyvec),
        shaped(valvec),
        shaped(logarithm_decay),
        shaped(write_rate),
        shaped(docids),
        prevdocs,
    )
    key_dim = keyvec.shape[2]
    value_dim = valvec.shape[2]
    identity_map = jnp.broadcast_to(
        jnp.eye(key_dim, dtype=jnp.float32)[None], (head_count, key_dim, key_dim)
    )
    zero_add = jnp.zeros((head_count, key_dim, value_dim), jnp.float32)

    def advance_block(prefix_pair, block_item):
        map_before, update_from_prior = prefix_pair
        local_output, query_effective, handed_operator, handed_update = block_item
        eff_now = jnp.einsum("htk,hkj->htj", query_effective, map_before, precision=PRECISE_PRODUCT)
        output_current = local_output + jnp.einsum(
            "cor,crm->com", query_effective, update_from_prior, precision=PRECISE_PRODUCT
        )
        map_after = jnp.einsum(
            "hkj,hjl->hkl", handed_operator, map_before, precision=PRECISE_PRODUCT
        )
        increment_later = (
            jnp.einsum(
                "ytn,yne->yte", handed_operator, update_from_prior, precision=PRECISE_PRODUCT
            )
            + handed_update
        )
        return ((map_after, increment_later), (eff_now, output_current))

    held, block_outs = next_latents(held, block_outs)
    local_output, query_effective, handed_operator, handed_update = block_outs
    slab_pair = (handed_operator[0], handed_update[0])
    effective_blocks, output_blocks = [query_effective[0]], [local_output[0]]
    for block in range(1, block_count):
        slab_pair, (eff_now, output_current) = advance_block(
            slab_pair,
            (local_output[block], query_effective[block], handed_operator[block], handed_update[block]),
        )
        effective_blocks.append(eff_now)
        output_blocks.append(output_current)
    effective_everything = jnp.stack(effective_blocks)
    output_everything = jnp.stack(output_blocks)
    held, slab_pair = next_latents(held, slab_pair)
    attend_group, group_count = latent_attention(
        mla_query, held, held_after, key_up, value_up, positions, docids, doc_starts, head_count
    )
    carried_in, mla_parts = incoming_state(slab_pair, slab_rows, attend_group, group_count)
    delta_attention_complete = output_everything + jnp.einsum(
        "enzx,nxu->enzu", effective_everything, carried_in, precision=PRECISE_PRODUCT
    )
    kda_out = (
        jnp.transpose(delta_attention_complete, (0, 2, 1, 3))
        .reshape(slab_rows, -1)
        .astype(jnp.bfloat16)
    )
    mla_out = jnp.concatenate(mla_parts, axis=1).reshape(slab_rows, -1)
    return (kda_out, mla_out)


def window_slabs_of(slab_rows):
    longest = lax.axis_size("ctx") * slab_rows // 2
    return -(-longest // slab_rows)


def carry_rounds(slab_rows):
    window = window_slabs_of(slab_rows)
    distance, rounds = 1, 2
    while 2 * distance < window:
        distance, rounds = 2 * distance, rounds + 1
    return rounds


def incoming_state(slab_pair, slab_rows, attend_group, group_count):
    map_now, add_now = slab_pair
    window = window_slabs_of(slab_rows)
    rounds = carry_rounds(slab_rows)
    groups_at = [[] for _ in range(rounds)]
    for group in range(group_count):
        groups_at[rounds - group_count + group if rounds > group_count else group * rounds // group_count].append(group)
    parts = []

    def exchange(value, distance, step):
        sent = lax.optimization_barrier(value.astype(jnp.bfloat16))
        got = shifted(sent, "ctx", distance)
        done = [attend_group(group, sent) for group in groups_at[step]]
        got, done = lax.optimization_barrier((got, done))
        parts.extend(done)
        return got.astype(jnp.float32)

    def product(left, right):
        return jnp.einsum("hkj,hjl->hkl", left, right, precision=PRECISE_PRODUCT)

    value_dim = add_now.shape[2]
    distance, step = 1, 0
    while 2 * distance < window:
        before = exchange(jnp.concatenate([add_now, map_now], axis=2), distance, step)
        joined = product(map_now, before)
        add_now = joined[:, :, :value_dim] + add_now
        map_now = joined[:, :, value_dim:]
        distance, step = 2 * distance, step + 1
    add_now = product(map_now, exchange(add_now, distance, step)) + add_now
    return exchange(add_now, 1, step + 1), parts


def latent_rounds(slab_rows):
    reach = min(window_slabs_of(slab_rows), lax.axis_size("ctx") - 1)
    plan, span = [], 1
    while 2 * span <= reach:
        plan.append((span, span))
        span *= 2
    if reach + 1 > span:
        plan.append((1, reach + 1 - span))
    return plan


def latent_round(held, slab_rows, step):
    distance, count = latent_rounds(slab_rows)[step]
    return jnp.concatenate([shifted(held[:count], "ctx", distance), held], axis=0)


def latent_attention(
    mla_query, held, held_after, key_up, value_up, positions, docids, doc_starts, head_count
):
    latents = held[-1]
    slab_rows = latents.shape[0]
    slabs = lax.axis_size("ctx")
    reach = min(window_slabs_of(slab_rows), slabs - 1)
    window_rows = (reach + 1) * slab_rows
    for step in range(len(latent_rounds(slab_rows)) - len(held_after)):
        held = latent_round(held, slab_rows, len(held_after) + step)
    key_rows = held.reshape(window_rows, latents.shape[1])
    key_first = (lax.axis_index("ctx") - reach) * slab_rows
    queries = mla_query.reshape(slab_rows, head_count, NOPE + ROPE)
    score_scale = 1.0 / math.sqrt(NOPE + ROPE)
    key_places = key_first + jnp.arange(window_rows, dtype=jnp.int32)
    key_docs = doc_of(key_places, doc_starts)
    allowed = (key_places[None, :] <= positions[:, None]) & (
        key_docs[None, :] == docids[:, None]
    )
    value_width = value_up.shape[1] // head_count
    group_count = carry_rounds(slab_rows)
    while head_count % group_count:
        group_count -= 1
    per_group = head_count // group_count

    def attend_group(group, tie):
        rows, _ = lax.optimization_barrier((key_rows, tie))
        heads = slice(group * per_group, (group + 1) * per_group)
        latent_part = rows[:, :LATENT]
        keys_nope = (
            jnp.dot(
                latent_part,
                key_up[:, group * per_group * NOPE : (group + 1) * per_group * NOPE],
                preferred_element_type=jnp.float32,
            )
            .astype(jnp.bfloat16)
            .reshape(window_rows, per_group, NOPE)
        )
        values = (
            jnp.dot(
                latent_part,
                value_up[
                    :, group * per_group * value_width : (group + 1) * per_group * value_width
                ],
                preferred_element_type=jnp.float32,
            )
            .astype(jnp.bfloat16)
            .reshape(window_rows, per_group, value_width)
        )
        scores = jnp.einsum(
            "thd,shd->hts",
            queries[:, heads, :NOPE],
            keys_nope,
            preferred_element_type=jnp.float32,
        )
        scores = (
            scores
            + jnp.einsum(
                "thr,sr->hts",
                queries[:, heads, NOPE:],
                rows[:, LATENT:],
                preferred_element_type=jnp.float32,
            )
        ) * score_scale
        masked = jnp.where(allowed[None], scores, -1e30)
        row_max = jnp.max(masked, axis=2, keepdims=True)
        weights = jnp.where(allowed[None], jnp.exp(masked - row_max), 0.0)
        row_total = jnp.sum(weights, axis=2)
        summed = jnp.einsum(
            "hts,shv->thv",
            weights.astype(jnp.bfloat16),
            values,
            preferred_element_type=jnp.float32,
        )
        return (summed / jnp.transpose(row_total)[:, :, None]).astype(jnp.bfloat16)

    return attend_group, group_count


def solution(mesh):
    in_specs = (
        P(("batch", "ctx"), None),
        P(("batch", "ctx"), None),
        P(("batch", "ctx"), None),
        P(("batch", "ctx"), None),
        P(("batch", "ctx"), None),
        P(("batch", "ctx"), None),
        P(("batch", "ctx"), None),
        P(),
        P(),
        P("batch"),
    )
    out_specs = (P(("batch", "ctx"), None), P(("batch", "ctx"), None))
    return jax.shard_map(local, mesh=mesh, in_specs=in_specs, out_specs=out_specs, check_vma=False)
```

```python
import math

import jax
import jax.numpy as jnp
from jax import lax
from jax.experimental import pallas as pl
from jax.experimental.pallas import tpu as pltpu
from jax.sharding import PartitionSpec as P

NOPE = 128
ROPE = 64
LATENT = 512
BLOCK = 64


PRECISE_PRODUCT = lax.Precision.HIGHEST


def prefix(array, axis, join, neutral):
    place = lax.axis_index(axis)
    gathered = jax.tree.map(
        lambda a, kind: lax.all_gather(a.astype(kind), axis),
        array,
        jax.tree.map(lambda a: jnp.bfloat16 if a.dtype == jnp.float32 else a.dtype, array),
    )
    state = jax.tree.map(lambda a, e: jnp.zeros_like(a) + jnp.asarray(e, a.dtype), array, neutral)

    def one(step, state):
        return join(
            state,
            jax.tree.map(
                lambda a, own: lax.dynamic_index_in_dim(a, step, 0, False).astype(own.dtype),
                gathered,
                array,
            ),
        )

    return lax.fori_loop(0, place, one, state)


def shifted(block, axis, distance):
    devices = range(lax.axis_size(axis))
    route = [(i - distance, i) for i in devices if i - distance in devices]
    return lax.ppermute(block, axis, route)


def unit_rows(values):
    return values * lax.rsqrt(jnp.sum(values * values, axis=-1, keepdims=True) + 1e-06)


def doc_of(positions, doc_starts):
    match_count = (doc_starts[None, :] <= positions[:, None]).astype(jnp.int32)
    return jnp.sum(match_count, axis=1) - 1


def unit_lower_inverse(strictly_lower):
    length = strictly_lower.shape[-1]
    identity = jnp.eye(length, dtype=jnp.float32)[None]
    result = identity - strictly_lower
    power_term = strictly_lower
    for level_index in range(length.bit_length() - 2):
        power_term = jnp.einsum("hij,hjk->hik", power_term, power_term, precision=PRECISE_PRODUCT)
        result = jnp.einsum(
            "hij,hjk->hik", result, identity + power_term, precision=PRECISE_PRODUCT
        )
    return result


def block_terms(query_unit, keyvec, valvec, logarithm_decay, write_gain, docids, prevdoc):
    length = docids.shape[0]
    cumulative = jnp.cumsum(logarithm_decay, axis=0)
    growth = jnp.exp(cumulative)
    key_plus = keyvec * growth
    key_minus = keyvec * jnp.exp(-cumulative)
    query_plus = query_unit * growth
    places = jnp.arange(length)
    same_doc = docids[:, None] == docids[None, :]
    strict = (places[:, None] > places[None, :]) & same_doc
    causal = (places[:, None] >= places[None, :]) & same_doc
    follow = (docids == prevdoc).astype(jnp.float32)
    inner_prod = jnp.einsum("thk,shk->hts", key_plus, key_minus, precision=PRECISE_PRODUCT)
    strictly_lower = (
        jnp.where(strict[None], inner_prod, 0.0) * jnp.transpose(write_gain)[:, :, None]
    )
    inverse = unit_lower_inverse(strictly_lower)
    value_rhs = jnp.transpose(valvec * write_gain[:, :, None], (1, 0, 2))
    key_rhs = jnp.transpose(key_plus * (write_gain * follow[:, None])[:, :, None], (1, 0, 2))
    value_solution = jnp.einsum("hts,hsv->htv", inverse, value_rhs, precision=PRECISE_PRODUCT)
    solved_key = jnp.einsum("hts,hsk->htk", inverse, key_rhs, precision=PRECISE_PRODUCT)
    mixing = jnp.where(
        causal[None],
        jnp.einsum("thk,shk->hts", query_plus, key_minus, precision=PRECISE_PRODUCT),
        0.0,
    )
    local_output = jnp.einsum("hts,hsv->htv", mixing, value_solution, precision=PRECISE_PRODUCT)
    query_effective = jnp.transpose(query_plus * follow[:, None, None], (1, 0, 2)) - jnp.einsum(
        "hts,hsk->htk", mixing, solved_key, precision=PRECISE_PRODUCT
    )
    last_doc = (docids == docids[length - 1]).astype(jnp.float32)
    key_trailing = (
        keyvec * jnp.exp(cumulative[length - 1][None] - cumulative) * last_doc[:, None, None]
    )
    growth_last = growth[length - 1]
    diagonal_map = growth_last[:, :, None] * jnp.eye(keyvec.shape[2], dtype=jnp.float32)[None]
    handed_operator = follow[length - 1] * diagonal_map - jnp.einsum(
        "shk,hsj->hkj", key_trailing, solved_key, precision=PRECISE_PRODUCT
    )
    handed_update = jnp.einsum(
        "omt,mor->mtr", key_trailing, value_solution, precision=PRECISE_PRODUCT
    )
    return (local_output, query_effective, handed_operator, handed_update)


def compose(prior_slab, successor_slab):
    joined_map = jnp.einsum(
        "hkj,hjl->hkl", successor_slab[0], prior_slab[0], precision=PRECISE_PRODUCT
    )
    combined_increment = (
        jnp.einsum("ytn,yne->yte", successor_slab[0], prior_slab[1], precision=PRECISE_PRODUCT)
        + successor_slab[1]
    )
    return (joined_map, combined_increment)


def local(
    kda_query,
    kda_key,
    kda_value,
    log_decay,
    write_rate,
    mla_query,
    latents,
    key_up,
    value_up,
    doc_lengths,
):
    slab_rows = latents.shape[0]
    head_count = write_rate.shape[1]
    first_row = lax.axis_index("ctx") * slab_rows
    doc_starts = jnp.cumsum(doc_lengths) - doc_lengths
    positions = first_row + jnp.arange(slab_rows, dtype=jnp.int32)
    docids = doc_of(positions, doc_starts)
    query_unit = unit_rows(kda_query.astype(jnp.float32).reshape(slab_rows, head_count, -1))
    keyvec = unit_rows(kda_key.astype(jnp.float32).reshape(slab_rows, head_count, -1))
    valvec = kda_value.astype(jnp.float32).reshape(slab_rows, head_count, -1)
    logarithm_decay = log_decay.astype(jnp.float32).reshape(slab_rows, head_count, -1)
    block_count = slab_rows // BLOCK
    prevdocs = doc_of(first_row + jnp.arange(block_count, dtype=jnp.int32) * BLOCK - 1, doc_starts)

    def shaped(values):
        return values.reshape((block_count, BLOCK) + values.shape[1:])

    block_outs = jax.vmap(block_terms)(
        shaped(query_unit),
        shaped(keyvec),
        shaped(valvec),
        shaped(logarithm_decay),
        shaped(write_rate),
        shaped(docids),
        prevdocs,
    )
    key_dim = keyvec.shape[2]
    value_dim = valvec.shape[2]
    identity_map = jnp.broadcast_to(
        jnp.eye(key_dim, dtype=jnp.float32)[None], (head_count, key_dim, key_dim)
    )
    zero_add = jnp.zeros((head_count, key_dim, value_dim), jnp.float32)

    def advance_block(prefix_pair, block_item):
        map_before, update_from_prior = prefix_pair
        local_output, query_effective, handed_operator, handed_update = block_item
        eff_now = jnp.einsum("htk,hkj->htj", query_effective, map_before, precision=PRECISE_PRODUCT)
        output_current = local_output + jnp.einsum(
            "cor,crm->com", query_effective, update_from_prior, precision=PRECISE_PRODUCT
        )
        map_after = jnp.einsum(
            "hkj,hjl->hkl", handed_operator, map_before, precision=PRECISE_PRODUCT
        )
        increment_later = (
            jnp.einsum(
                "ytn,yne->yte", handed_operator, update_from_prior, precision=PRECISE_PRODUCT
            )
            + handed_update
        )
        return ((map_after, increment_later), (eff_now, output_current))

    local_output, query_effective, handed_operator, handed_update = block_outs
    slab_pair = (handed_operator[0], handed_update[0])
    effective_blocks, output_blocks = [query_effective[0]], [local_output[0]]
    for block in range(1, block_count):
        slab_pair, (eff_now, output_current) = advance_block(
            slab_pair,
            (local_output[block], query_effective[block], handed_operator[block], handed_update[block]),
        )
        effective_blocks.append(eff_now)
        output_blocks.append(output_current)
    effective_everything = jnp.stack(effective_blocks)
    output_everything = jnp.stack(output_blocks)
    attend_group, group_count = latent_attention(
        mla_query, latents, key_up, value_up, positions, docids, doc_starts, head_count
    )
    carried_in, mla_parts = incoming_state(slab_pair, slab_rows, attend_group, group_count)
    delta_attention_complete = output_everything + jnp.einsum(
        "enzx,nxu->enzu", effective_everything, carried_in, precision=PRECISE_PRODUCT
    )
    kda_out = (
        jnp.transpose(delta_attention_complete, (0, 2, 1, 3))
        .reshape(slab_rows, -1)
        .astype(jnp.bfloat16)
    )
    mla_out = jnp.concatenate(mla_parts, axis=1)
    return (kda_out, mla_out)


def window_slabs_of(slab_rows):
    longest = lax.axis_size("ctx") * slab_rows // 2
    return -(-longest // slab_rows)


def carry_rounds(slab_rows):
    window = window_slabs_of(slab_rows)
    distance, rounds = 1, 2
    while 2 * distance < window:
        distance, rounds = 2 * distance, rounds + 1
    return rounds


def incoming_state(slab_pair, slab_rows, attend_group, group_count):
    map_now, add_now = slab_pair
    window = window_slabs_of(slab_rows)
    rounds = carry_rounds(slab_rows)
    groups_at = [[] for _ in range(rounds)]
    for group in range(group_count):
        groups_at[rounds - group_count + group if rounds > group_count else group * rounds // group_count].append(group)
    parts = []

    def exchange(value, distance, step):
        sent = lax.optimization_barrier(value.astype(jnp.bfloat16))
        got = shifted(sent, "ctx", distance)
        done = [attend_group(group, sent) for group in groups_at[step]]
        got, done = lax.optimization_barrier((got, done))
        parts.extend(done)
        return got.astype(jnp.float32)

    def product(left, right):
        return jnp.einsum("hkj,hjl->hkl", left, right, precision=PRECISE_PRODUCT)

    value_dim = add_now.shape[2]
    distance, step = 1, 0
    while 2 * distance < window:
        before = exchange(jnp.concatenate([add_now, map_now], axis=2), distance, step)
        joined = product(map_now, before)
        add_now = joined[:, :, :value_dim] + add_now
        map_now = joined[:, :, value_dim:]
        distance, step = 2 * distance, step + 1
    add_now = product(map_now, exchange(add_now, distance, step)) + add_now
    return exchange(add_now, 1, step + 1), parts


def attend_body(scale, qn_ref, qr_ref, kn_ref, kr_ref, v_ref, allowed_ref, out_ref):
    allowed = allowed_ref[...] != 0
    keys_rope = kr_ref[...]
    for head in range(qn_ref.shape[0]):
        columns = slice(head * NOPE, (head + 1) * NOPE)
        contract = (((1,), (1,)), ((), ()))
        scores = lax.dot_general(
            qn_ref[head], kn_ref[:, columns], contract, preferred_element_type=jnp.float32
        )
        scores = (
            scores
            + lax.dot_general(
                qr_ref[head], keys_rope, contract, preferred_element_type=jnp.float32
            )
        ) * scale
        masked = jnp.where(allowed, scores, -1e30)
        row_max = jnp.max(masked, axis=1, keepdims=True)
        weights = jnp.where(allowed, jnp.exp(masked - row_max), 0.0)
        row_total = jnp.sum(weights, axis=1, keepdims=True)
        summed = jnp.dot(
            weights.astype(jnp.bfloat16), v_ref[:, columns], preferred_element_type=jnp.float32
        )
        out_ref[:, columns] = (summed / row_total).astype(out_ref.dtype)


def attend_kernel(query_nope, query_rope, keys_nope, keys_rope, values, allowed, scale):
    heads, rows, _ = query_nope.shape
    window = keys_nope.shape[0]
    flops = 2 * heads * rows * window * (NOPE + ROPE + values.shape[1] // heads)
    return pl.pallas_call(
        lambda *refs: attend_body(scale, *refs),
        out_shape=jax.ShapeDtypeStruct((rows, values.shape[1]), jnp.bfloat16),
        in_specs=[pl.BlockSpec(memory_space=pltpu.VMEM)] * 6,
        out_specs=pl.BlockSpec(memory_space=pltpu.VMEM),
        cost_estimate=pl.CostEstimate(
            flops=flops,
            transcendentals=heads * rows * window,
            bytes_accessed=2 * window * (keys_nope.shape[1] + values.shape[1] + ROPE)
            + 4 * rows * window,
        ),
    )(query_nope, query_rope, keys_nope, keys_rope, values, allowed)


def latent_attention(
    mla_query, latents, key_up, value_up, positions, docids, doc_starts, head_count
):
    slab_rows = latents.shape[0]
    slabs = lax.axis_size("ctx")
    reach = window_slabs_of(slab_rows)
    window_slabs = min(reach + 1, slabs)
    window_rows = window_slabs * slab_rows
    everything = lax.all_gather(latents, "ctx", tiled=True)
    first_slab = jnp.clip(lax.axis_index("ctx") - reach, 0, slabs - window_slabs)
    key_first = first_slab * slab_rows
    key_rows = lax.dynamic_slice_in_dim(everything, key_first, window_rows, 0)
    queries = mla_query.reshape(slab_rows, head_count, NOPE + ROPE)
    score_scale = 1.0 / math.sqrt(NOPE + ROPE)
    key_places = key_first + jnp.arange(window_rows, dtype=jnp.int32)
    key_docs = doc_of(key_places, doc_starts)
    allowed = (key_places[None, :] <= positions[:, None]) & (
        key_docs[None, :] == docids[:, None]
    )
    allowed_flags = allowed.astype(jnp.int32)
    value_width = value_up.shape[1] // head_count
    group_count = carry_rounds(slab_rows)
    while head_count % group_count:
        group_count -= 1
    per_group = head_count // group_count

    def attend_group(group, tie):
        rows, _ = lax.optimization_barrier((key_rows, tie))
        heads = slice(group * per_group, (group + 1) * per_group)
        latent_part = rows[:, :LATENT]
        keys_nope = (
            jnp.dot(
                latent_part,
                key_up[:, group * per_group * NOPE : (group + 1) * per_group * NOPE],
                preferred_element_type=jnp.float32,
            )
            .astype(jnp.bfloat16)
            .reshape(window_rows, per_group, NOPE)
        )
        values = (
            jnp.dot(
                latent_part,
                value_up[
                    :, group * per_group * value_width : (group + 1) * per_group * value_width
                ],
                preferred_element_type=jnp.float32,
            )
            .astype(jnp.bfloat16)
            .reshape(window_rows, per_group, value_width)
        )
        return attend_kernel(
            jnp.transpose(queries[:, heads, :NOPE], (1, 0, 2)),
            jnp.transpose(queries[:, heads, NOPE:], (1, 0, 2)),
            keys_nope.reshape(window_rows, -1),
            rows[:, LATENT:],
            values.reshape(window_rows, -1),
            allowed_flags,
            score_scale,
        )

    return attend_group, group_count


def solution(mesh):
    in_specs = (
        P(("batch", "ctx"), None),
        P(("batch", "ctx"), None),
        P(("batch", "ctx"), None),
        P(("batch", "ctx"), None),
        P(("batch", "ctx"), None),
        P(("batch", "ctx"), None),
        P(("batch", "ctx"), None),
        P(),
        P(),
        P("batch"),
    )
    out_specs = (P(("batch", "ctx"), None), P(("batch", "ctx"), None))
    return jax.shard_map(local, mesh=mesh, in_specs=in_specs, out_specs=out_specs, check_vma=False)
```

```python
import math

import jax
import jax.numpy as jnp
from jax import lax
from jax.sharding import PartitionSpec as P

NOPE = 128
ROPE = 64
LATENT = 512
BLOCK = 64


PRECISE_PRODUCT = lax.Precision.HIGHEST


def prefix(array, axis, join, neutral):
    place = lax.axis_index(axis)
    gathered = jax.tree.map(
        lambda a, kind: lax.all_gather(a.astype(kind), axis),
        array,
        jax.tree.map(lambda a: jnp.bfloat16 if a.dtype == jnp.float32 else a.dtype, array),
    )
    state = jax.tree.map(lambda a, e: jnp.zeros_like(a) + jnp.asarray(e, a.dtype), array, neutral)

    def one(step, state):
        return join(
            state,
            jax.tree.map(
                lambda a, own: lax.dynamic_index_in_dim(a, step, 0, False).astype(own.dtype),
                gathered,
                array,
            ),
        )

    return lax.fori_loop(0, place, one, state)


def shifted(block, axis, distance):
    devices = range(lax.axis_size(axis))
    route = [(i - distance, i) for i in devices if i - distance in devices]
    return lax.ppermute(block, axis, route)


def unit_rows(values):
    return values * lax.rsqrt(jnp.sum(values * values, axis=-1, keepdims=True) + 1e-06)


def doc_of(positions, doc_starts):
    match_count = (doc_starts[None, :] <= positions[:, None]).astype(jnp.int32)
    return jnp.sum(match_count, axis=1) - 1


def unit_lower_inverse(strictly_lower):
    length = strictly_lower.shape[-1]
    identity = jnp.eye(length, dtype=jnp.float32)[None]
    result = identity - strictly_lower
    power_term = strictly_lower
    for level_index in range(length.bit_length() - 2):
        power_term = jnp.einsum("hij,hjk->hik", power_term, power_term, precision=PRECISE_PRODUCT)
        result = jnp.einsum(
            "hij,hjk->hik", result, identity + power_term, precision=PRECISE_PRODUCT
        )
    return result


def block_terms(query_unit, keyvec, valvec, logarithm_decay, write_gain, docids, prevdoc):
    length = docids.shape[0]
    cumulative = jnp.cumsum(logarithm_decay, axis=0)
    growth = jnp.exp(cumulative)
    key_plus = keyvec * growth
    key_minus = keyvec * jnp.exp(-cumulative)
    query_plus = query_unit * growth
    places = jnp.arange(length)
    same_doc = docids[:, None] == docids[None, :]
    strict = (places[:, None] > places[None, :]) & same_doc
    causal = (places[:, None] >= places[None, :]) & same_doc
    follow = (docids == prevdoc).astype(jnp.float32)
    inner_prod = jnp.einsum("thk,shk->hts", key_plus, key_minus, precision=PRECISE_PRODUCT)
    strictly_lower = (
        jnp.where(strict[None], inner_prod, 0.0) * jnp.transpose(write_gain)[:, :, None]
    )
    inverse = unit_lower_inverse(strictly_lower)
    value_rhs = jnp.transpose(valvec * write_gain[:, :, None], (1, 0, 2))
    key_rhs = jnp.transpose(key_plus * (write_gain * follow[:, None])[:, :, None], (1, 0, 2))
    value_solution = jnp.einsum("hts,hsv->htv", inverse, value_rhs, precision=PRECISE_PRODUCT)
    solved_key = jnp.einsum("hts,hsk->htk", inverse, key_rhs, precision=PRECISE_PRODUCT)
    mixing = jnp.where(
        causal[None],
        jnp.einsum("thk,shk->hts", query_plus, key_minus, precision=PRECISE_PRODUCT),
        0.0,
    )
    local_output = jnp.einsum("hts,hsv->htv", mixing, value_solution, precision=PRECISE_PRODUCT)
    query_effective = jnp.transpose(query_plus * follow[:, None, None], (1, 0, 2)) - jnp.einsum(
        "hts,hsk->htk", mixing, solved_key, precision=PRECISE_PRODUCT
    )
    last_doc = (docids == docids[length - 1]).astype(jnp.float32)
    key_trailing = (
        keyvec * jnp.exp(cumulative[length - 1][None] - cumulative) * last_doc[:, None, None]
    )
    growth_last = growth[length - 1]
    diagonal_map = growth_last[:, :, None] * jnp.eye(keyvec.shape[2], dtype=jnp.float32)[None]
    handed_operator = follow[length - 1] * diagonal_map - jnp.einsum(
        "shk,hsj->hkj", key_trailing, solved_key, precision=PRECISE_PRODUCT
    )
    handed_update = jnp.einsum(
        "omt,mor->mtr", key_trailing, value_solution, precision=PRECISE_PRODUCT
    )
    return (local_output, query_effective, handed_operator, handed_update)


def compose(prior_slab, successor_slab):
    joined_map = jnp.einsum(
        "hkj,hjl->hkl", successor_slab[0], prior_slab[0], precision=PRECISE_PRODUCT
    )
    combined_increment = (
        jnp.einsum("ytn,yne->yte", successor_slab[0], prior_slab[1], precision=PRECISE_PRODUCT)
        + successor_slab[1]
    )
    return (joined_map, combined_increment)


def local(
    kda_query,
    kda_key,
    kda_value,
    log_decay,
    write_rate,
    mla_query,
    latents,
    key_up,
    value_up,
    doc_lengths,
):
    slab_rows = latents.shape[0]
    head_count = write_rate.shape[1]
    first_row = lax.axis_index("ctx") * slab_rows
    doc_starts = jnp.cumsum(doc_lengths) - doc_lengths
    positions = first_row + jnp.arange(slab_rows, dtype=jnp.int32)
    docids = doc_of(positions, doc_starts)
    query_unit = unit_rows(kda_query.astype(jnp.float32).reshape(slab_rows, head_count, -1))
    keyvec = unit_rows(kda_key.astype(jnp.float32).reshape(slab_rows, head_count, -1))
    valvec = kda_value.astype(jnp.float32).reshape(slab_rows, head_count, -1)
    logarithm_decay = log_decay.astype(jnp.float32).reshape(slab_rows, head_count, -1)
    block_count = slab_rows // BLOCK
    prevdocs = doc_of(first_row + jnp.arange(block_count, dtype=jnp.int32) * BLOCK - 1, doc_starts)

    def shaped(values):
        return values.reshape((block_count, BLOCK) + values.shape[1:])

    block_outs = jax.vmap(block_terms)(
        shaped(query_unit),
        shaped(keyvec),
        shaped(valvec),
        shaped(logarithm_decay),
        shaped(write_rate),
        shaped(docids),
        prevdocs,
    )
    key_dim = keyvec.shape[2]
    value_dim = valvec.shape[2]
    identity_map = jnp.broadcast_to(
        jnp.eye(key_dim, dtype=jnp.float32)[None], (head_count, key_dim, key_dim)
    )
    zero_add = jnp.zeros((head_count, key_dim, value_dim), jnp.float32)

    def advance_block(prefix_pair, block_item):
        map_before, update_from_prior = prefix_pair
        local_output, query_effective, handed_operator, handed_update = block_item
        eff_now = jnp.einsum("htk,hkj->htj", query_effective, map_before, precision=PRECISE_PRODUCT)
        output_current = local_output + jnp.einsum(
            "cor,crm->com", query_effective, update_from_prior, precision=PRECISE_PRODUCT
        )
        map_after = jnp.einsum(
            "hkj,hjl->hkl", handed_operator, map_before, precision=PRECISE_PRODUCT
        )
        increment_later = (
            jnp.einsum(
                "ytn,yne->yte", handed_operator, update_from_prior, precision=PRECISE_PRODUCT
            )
            + handed_update
        )
        return ((map_after, increment_later), (eff_now, output_current))

    local_output, query_effective, handed_operator, handed_update = block_outs
    slab_pair = (handed_operator[0], handed_update[0])
    effective_blocks, output_blocks = [query_effective[0]], [local_output[0]]
    for block in range(1, block_count):
        slab_pair, (eff_now, output_current) = advance_block(
            slab_pair,
            (local_output[block], query_effective[block], handed_operator[block], handed_update[block]),
        )
        effective_blocks.append(eff_now)
        output_blocks.append(output_current)
    effective_everything = jnp.stack(effective_blocks)
    output_everything = jnp.stack(output_blocks)
    attend_group, group_count, latents_ready = latent_attention(
        mla_query, latents, key_up, value_up, positions, docids, doc_starts, head_count
    )
    carried_in, mla_parts = incoming_state(
        slab_pair, slab_rows, attend_group, group_count, latents_ready
    )
    delta_attention_complete = output_everything + jnp.einsum(
        "enzx,nxu->enzu", effective_everything, carried_in, precision=PRECISE_PRODUCT
    )
    kda_out = (
        jnp.transpose(delta_attention_complete, (0, 2, 1, 3))
        .reshape(slab_rows, -1)
        .astype(jnp.bfloat16)
    )
    mla_out = jnp.concatenate(mla_parts, axis=1).reshape(slab_rows, -1)
    return (kda_out, mla_out)


def window_slabs_of(slab_rows):
    longest = lax.axis_size("ctx") * slab_rows // 2
    return -(-longest // slab_rows)


def carry_rounds(slab_rows):
    window = window_slabs_of(slab_rows)
    distance, rounds = 1, 2
    while 2 * distance < window:
        distance, rounds = 2 * distance, rounds + 1
    return rounds


def incoming_state(slab_pair, slab_rows, attend_group, group_count, latents_ready):
    map_now, add_now = slab_pair
    window = window_slabs_of(slab_rows)
    rounds = carry_rounds(slab_rows)
    groups_at = [[] for _ in range(rounds)]
    for group in range(group_count):
        groups_at[group * rounds // group_count].append(group)
    parts = []

    def exchange(value, distance, step):
        sent = value.astype(jnp.bfloat16)
        if step == 0:
            sent = latents_ready(sent)
        sent = lax.optimization_barrier(sent)
        got = shifted(sent, "ctx", distance)
        done = [attend_group(group, sent) for group in groups_at[step]]
        got, done = lax.optimization_barrier((got, done))
        parts.extend(done)
        return got.astype(jnp.float32)

    def product(left, right):
        return jnp.einsum("hkj,hjl->hkl", left, right, precision=PRECISE_PRODUCT)

    value_dim = add_now.shape[2]
    distance, step = 1, 0
    while 2 * distance < window:
        before = exchange(jnp.concatenate([add_now, map_now], axis=2), distance, step)
        joined = product(map_now, before)
        add_now = joined[:, :, :value_dim] + add_now
        map_now = joined[:, :, value_dim:]
        distance, step = 2 * distance, step + 1
    add_now = product(map_now, exchange(add_now, distance, step)) + add_now
    return exchange(add_now, 1, step + 1), parts


def latent_attention(
    mla_query, latents, key_up, value_up, positions, docids, doc_starts, head_count
):
    slab_rows = latents.shape[0]
    slabs = lax.axis_size("ctx")
    reach = window_slabs_of(slab_rows)
    window_slabs = min(reach + 1, slabs)
    window_rows = window_slabs * slab_rows
    everything = lax.all_gather(latents, "ctx", tiled=True)
    first_slab = jnp.clip(lax.axis_index("ctx") - reach, 0, slabs - window_slabs)
    key_first = first_slab * slab_rows
    key_rows = lax.dynamic_slice_in_dim(everything, key_first, window_rows, 0)
    queries = mla_query.reshape(slab_rows, head_count, NOPE + ROPE)
    score_scale = 1.0 / math.sqrt(NOPE + ROPE)
    key_places = key_first + jnp.arange(window_rows, dtype=jnp.int32)
    key_docs = doc_of(key_places, doc_starts)
    allowed = (key_places[None, :] <= positions[:, None]) & (
        key_docs[None, :] == docids[:, None]
    )
    value_width = value_up.shape[1] // head_count
    group_count = carry_rounds(slab_rows)
    while head_count % group_count:
        group_count -= 1
    per_group = head_count // group_count

    def attend_group(group, tie):
        rows, _ = lax.optimization_barrier((key_rows, tie))
        heads = slice(group * per_group, (group + 1) * per_group)
        latent_part = rows[:, :LATENT]
        keys_nope = (
            jnp.dot(
                latent_part,
                key_up[:, group * per_group * NOPE : (group + 1) * per_group * NOPE],
                preferred_element_type=jnp.float32,
            )
            .astype(jnp.bfloat16)
            .reshape(window_rows, per_group, NOPE)
        )
        values = (
            jnp.dot(
                latent_part,
                value_up[
                    :, group * per_group * value_width : (group + 1) * per_group * value_width
                ],
                preferred_element_type=jnp.float32,
            )
            .astype(jnp.bfloat16)
            .reshape(window_rows, per_group, value_width)
        )
        scores = jnp.einsum(
            "thd,shd->hts",
            queries[:, heads, :NOPE],
            keys_nope,
            preferred_element_type=jnp.float32,
        )
        scores = (
            scores
            + jnp.einsum(
                "thr,sr->hts",
                queries[:, heads, NOPE:],
                rows[:, LATENT:],
                preferred_element_type=jnp.float32,
            )
        ) * score_scale
        masked = jnp.where(allowed[None], scores, -1e30)
        row_max = jnp.max(masked, axis=2, keepdims=True)
        weights = jnp.where(allowed[None], jnp.exp(masked - row_max), 0.0)
        row_total = jnp.sum(weights, axis=2)
        summed = jnp.einsum(
            "hts,shv->thv",
            weights.astype(jnp.bfloat16),
            values,
            preferred_element_type=jnp.float32,
        )
        return (summed / jnp.transpose(row_total)[:, :, None]).astype(jnp.bfloat16)

    def latents_ready(value):
        return lax.optimization_barrier((key_rows, value))[1]

    return attend_group, group_count, latents_ready


def solution(mesh):
    in_specs = (
        P(("batch", "ctx"), None),
        P(("batch", "ctx"), None),
        P(("batch", "ctx"), None),
        P(("batch", "ctx"), None),
        P(("batch", "ctx"), None),
        P(("batch", "ctx"), None),
        P(("batch", "ctx"), None),
        P(),
        P(),
        P("batch"),
    )
    out_specs = (P(("batch", "ctx"), None), P(("batch", "ctx"), None))
    return jax.shard_map(local, mesh=mesh, in_specs=in_specs, out_specs=out_specs, check_vma=False)
```

```python
import math

import jax
import jax.numpy as jnp
from jax import lax
from jax.experimental import pallas as pl
from jax.experimental.pallas import tpu as pltpu
from jax.sharding import PartitionSpec as P

NOPE = 128
ROPE = 64
LATENT = 512
BLOCK = 64


PRECISE_PRODUCT = lax.Precision.HIGHEST


def prefix(array, axis, join, neutral):
    place = lax.axis_index(axis)
    gathered = jax.tree.map(
        lambda a, kind: lax.all_gather(a.astype(kind), axis),
        array,
        jax.tree.map(lambda a: jnp.bfloat16 if a.dtype == jnp.float32 else a.dtype, array),
    )
    state = jax.tree.map(lambda a, e: jnp.zeros_like(a) + jnp.asarray(e, a.dtype), array, neutral)

    def one(step, state):
        return join(
            state,
            jax.tree.map(
                lambda a, own: lax.dynamic_index_in_dim(a, step, 0, False).astype(own.dtype),
                gathered,
                array,
            ),
        )

    return lax.fori_loop(0, place, one, state)


def shifted(block, axis, distance):
    devices = range(lax.axis_size(axis))
    route = [(i - distance, i) for i in devices if i - distance in devices]
    return lax.ppermute(block, axis, route)


def unit_rows(values):
    return values * lax.rsqrt(jnp.sum(values * values, axis=-1, keepdims=True) + 1e-06)


def doc_of(positions, doc_starts):
    match_count = (doc_starts[None, :] <= positions[:, None]).astype(jnp.int32)
    return jnp.sum(match_count, axis=1) - 1


def unit_lower_inverse(strictly_lower):
    length = strictly_lower.shape[-1]
    identity = jnp.eye(length, dtype=jnp.float32)[None]
    result = identity - strictly_lower
    power_term = strictly_lower
    for level_index in range(length.bit_length() - 2):
        power_term = jnp.einsum("hij,hjk->hik", power_term, power_term, precision=PRECISE_PRODUCT)
        result = jnp.einsum(
            "hij,hjk->hik", result, identity + power_term, precision=PRECISE_PRODUCT
        )
    return result


def block_terms(query_unit, keyvec, valvec, logarithm_decay, write_gain, docids, prevdoc):
    length = docids.shape[0]
    cumulative = jnp.cumsum(logarithm_decay, axis=0)
    growth = jnp.exp(cumulative)
    key_plus = keyvec * growth
    key_minus = keyvec * jnp.exp(-cumulative)
    query_plus = query_unit * growth
    places = jnp.arange(length)
    same_doc = docids[:, None] == docids[None, :]
    strict = (places[:, None] > places[None, :]) & same_doc
    causal = (places[:, None] >= places[None, :]) & same_doc
    follow = (docids == prevdoc).astype(jnp.float32)
    inner_prod = jnp.einsum("thk,shk->hts", key_plus, key_minus, precision=PRECISE_PRODUCT)
    strictly_lower = (
        jnp.where(strict[None], inner_prod, 0.0) * jnp.transpose(write_gain)[:, :, None]
    )
    inverse = lax.optimization_barrier(unit_lower_inverse(strictly_lower))
    value_rhs = jnp.transpose(valvec * write_gain[:, :, None], (1, 0, 2))
    key_rhs = jnp.transpose(key_plus * (write_gain * follow[:, None])[:, :, None], (1, 0, 2))
    value_solution = jnp.einsum("hts,hsv->htv", inverse, value_rhs, precision=PRECISE_PRODUCT)
    solved_key = jnp.einsum("hts,hsk->htk", inverse, key_rhs, precision=PRECISE_PRODUCT)
    mixing = jnp.where(
        causal[None],
        jnp.einsum("thk,shk->hts", query_plus, key_minus, precision=PRECISE_PRODUCT),
        0.0,
    )
    local_output = jnp.einsum("hts,hsv->htv", mixing, value_solution, precision=PRECISE_PRODUCT)
    query_effective = jnp.transpose(query_plus * follow[:, None, None], (1, 0, 2)) - jnp.einsum(
        "hts,hsk->htk", mixing, solved_key, precision=PRECISE_PRODUCT
    )
    last_doc = (docids == docids[length - 1]).astype(jnp.float32)
    key_trailing = (
        keyvec * jnp.exp(cumulative[length - 1][None] - cumulative) * last_doc[:, None, None]
    )
    growth_last = growth[length - 1]
    diagonal_map = growth_last[:, :, None] * jnp.eye(keyvec.shape[2], dtype=jnp.float32)[None]
    handed_operator = follow[length - 1] * diagonal_map - jnp.einsum(
        "shk,hsj->hkj", key_trailing, solved_key, precision=PRECISE_PRODUCT
    )
    handed_update = jnp.einsum(
        "omt,mor->mtr", key_trailing, value_solution, precision=PRECISE_PRODUCT
    )
    return (local_output, query_effective, handed_operator, handed_update)


def compose(prior_slab, successor_slab):
    joined_map = jnp.einsum(
        "hkj,hjl->hkl", successor_slab[0], prior_slab[0], precision=PRECISE_PRODUCT
    )
    combined_increment = (
        jnp.einsum("ytn,yne->yte", successor_slab[0], prior_slab[1], precision=PRECISE_PRODUCT)
        + successor_slab[1]
    )
    return (joined_map, combined_increment)


def local(
    kda_query,
    kda_key,
    kda_value,
    log_decay,
    write_rate,
    mla_query,
    latents,
    key_up,
    value_up,
    doc_lengths,
):
    slab_rows = latents.shape[0]
    head_count = write_rate.shape[1]
    first_row = lax.axis_index("ctx") * slab_rows
    doc_starts = jnp.cumsum(doc_lengths) - doc_lengths
    positions = first_row + jnp.arange(slab_rows, dtype=jnp.int32)
    docids = doc_of(positions, doc_starts)
    query_unit = unit_rows(kda_query.astype(jnp.float32).reshape(slab_rows, head_count, -1))
    keyvec = unit_rows(kda_key.astype(jnp.float32).reshape(slab_rows, head_count, -1))
    valvec = kda_value.astype(jnp.float32).reshape(slab_rows, head_count, -1)
    logarithm_decay = log_decay.astype(jnp.float32).reshape(slab_rows, head_count, -1)
    block_count = slab_rows // BLOCK
    prevdocs = doc_of(first_row + jnp.arange(block_count, dtype=jnp.int32) * BLOCK - 1, doc_starts)

    def shaped(values):
        return values.reshape((block_count, BLOCK) + values.shape[1:])

    block_outs = jax.vmap(block_terms)(
        shaped(query_unit),
        shaped(keyvec),
        shaped(valvec),
        shaped(logarithm_decay),
        shaped(write_rate),
        shaped(docids),
        prevdocs,
    )
    key_dim = keyvec.shape[2]
    value_dim = valvec.shape[2]
    identity_map = jnp.broadcast_to(
        jnp.eye(key_dim, dtype=jnp.float32)[None], (head_count, key_dim, key_dim)
    )
    zero_add = jnp.zeros((head_count, key_dim, value_dim), jnp.float32)

    def advance_block(prefix_pair, block_item):
        map_before, update_from_prior = prefix_pair
        local_output, query_effective, handed_operator, handed_update = block_item
        eff_now = jnp.einsum("htk,hkj->htj", query_effective, map_before, precision=PRECISE_PRODUCT)
        output_current = local_output + jnp.einsum(
            "cor,crm->com", query_effective, update_from_prior, precision=PRECISE_PRODUCT
        )
        map_after = jnp.einsum(
            "hkj,hjl->hkl", handed_operator, map_before, precision=PRECISE_PRODUCT
        )
        increment_later = (
            jnp.einsum(
                "ytn,yne->yte", handed_operator, update_from_prior, precision=PRECISE_PRODUCT
            )
            + handed_update
        )
        return ((map_after, increment_later), (eff_now, output_current))

    local_output, query_effective, handed_operator, handed_update = block_outs
    slab_pair = (handed_operator[0], handed_update[0])
    effective_blocks, output_blocks = [query_effective[0]], [local_output[0]]
    for block in range(1, block_count):
        slab_pair, (eff_now, output_current) = advance_block(
            slab_pair,
            (local_output[block], query_effective[block], handed_operator[block], handed_update[block]),
        )
        effective_blocks.append(eff_now)
        output_blocks.append(output_current)
    effective_everything = jnp.stack(effective_blocks)
    output_everything = jnp.stack(output_blocks)
    attend_group, group_count, latents_ready = latent_attention(
        mla_query, latents, key_up, value_up, positions, docids, doc_starts, head_count
    )
    carried_in, mla_parts = incoming_state(
        slab_pair, slab_rows, attend_group, group_count, latents_ready
    )
    delta_attention_complete = output_everything + jnp.einsum(
        "enzx,nxu->enzu", effective_everything, carried_in, precision=PRECISE_PRODUCT
    )
    kda_out = (
        jnp.transpose(delta_attention_complete, (0, 2, 1, 3))
        .reshape(slab_rows, -1)
        .astype(jnp.bfloat16)
    )
    mla_out = jnp.concatenate(mla_parts, axis=1)
    return (kda_out, mla_out)


def window_slabs_of(slab_rows):
    longest = lax.axis_size("ctx") * slab_rows // 2
    return -(-longest // slab_rows)


def carry_rounds(slab_rows):
    window = window_slabs_of(slab_rows)
    distance, rounds = 1, 2
    while 2 * distance < window:
        distance, rounds = 2 * distance, rounds + 1
    return rounds


def incoming_state(slab_pair, slab_rows, attend_group, group_count, latents_ready):
    map_now, add_now = slab_pair
    window = window_slabs_of(slab_rows)
    rounds = carry_rounds(slab_rows)
    groups_at = [[] for _ in range(rounds)]
    for group in range(group_count):
        groups_at[group * rounds // group_count].append(group)
    parts = []

    def exchange(value, distance, step):
        sent = value.astype(jnp.bfloat16)
        if step == 0:
            sent = latents_ready(sent)
        sent = lax.optimization_barrier(sent)
        got = shifted(sent, "ctx", distance)
        done = [attend_group(group, sent) for group in groups_at[step]]
        got, done = lax.optimization_barrier((got, done))
        parts.extend(done)
        return got.astype(jnp.float32)

    def product(left, right):
        return jnp.einsum("hkj,hjl->hkl", left, right, precision=PRECISE_PRODUCT)

    value_dim = add_now.shape[2]
    distance, step = 1, 0
    while 2 * distance < window:
        before = exchange(jnp.concatenate([add_now, map_now], axis=2), distance, step)
        joined = product(map_now, before)
        add_now = joined[:, :, :value_dim] + add_now
        map_now = joined[:, :, value_dim:]
        distance, step = 2 * distance, step + 1
    add_now = product(map_now, exchange(add_now, distance, step)) + add_now
    return exchange(add_now, 1, step + 1), parts


def attend_body(scale, qn_ref, qr_ref, kn_ref, kr_ref, v_ref, allowed_ref, out_ref):
    allowed = allowed_ref[...] != 0
    keys_rope = kr_ref[...]
    for head in range(qn_ref.shape[0]):
        columns = slice(head * NOPE, (head + 1) * NOPE)
        contract = (((1,), (1,)), ((), ()))
        scores = lax.dot_general(
            qn_ref[head], kn_ref[:, columns], contract, preferred_element_type=jnp.float32
        )
        scores = (
            scores
            + lax.dot_general(
                qr_ref[head], keys_rope, contract, preferred_element_type=jnp.float32
            )
        ) * scale
        masked = jnp.where(allowed, scores, -1e30)
        row_max = jnp.max(masked, axis=1, keepdims=True)
        weights = jnp.where(allowed, jnp.exp(masked - row_max), 0.0)
        row_total = jnp.sum(weights, axis=1, keepdims=True)
        summed = jnp.dot(
            weights.astype(jnp.bfloat16), v_ref[:, columns], preferred_element_type=jnp.float32
        )
        out_ref[:, columns] = (summed / row_total).astype(out_ref.dtype)


def attend_kernel(query_nope, query_rope, keys_nope, keys_rope, values, allowed, scale):
    heads, rows, _ = query_nope.shape
    window = keys_nope.shape[0]
    flops = 2 * heads * rows * window * (NOPE + ROPE + values.shape[1] // heads)
    return pl.pallas_call(
        lambda *refs: attend_body(scale, *refs),
        out_shape=jax.ShapeDtypeStruct((rows, values.shape[1]), jnp.bfloat16),
        in_specs=[pl.BlockSpec(memory_space=pltpu.VMEM)] * 6,
        out_specs=pl.BlockSpec(memory_space=pltpu.VMEM),
        cost_estimate=pl.CostEstimate(
            flops=flops,
            transcendentals=heads * rows * window,
            bytes_accessed=2 * window * (keys_nope.shape[1] + values.shape[1] + ROPE)
            + 4 * rows * window,
        ),
    )(query_nope, query_rope, keys_nope, keys_rope, values, allowed)


def latent_attention(
    mla_query, latents, key_up, value_up, positions, docids, doc_starts, head_count
):
    slab_rows = latents.shape[0]
    slabs = lax.axis_size("ctx")
    reach = window_slabs_of(slab_rows)
    window_slabs = min(reach + 1, slabs)
    window_rows = window_slabs * slab_rows
    everything = lax.all_gather(latents, "ctx", tiled=True)
    first_slab = jnp.clip(lax.axis_index("ctx") - reach, 0, slabs - window_slabs)
    key_first = first_slab * slab_rows
    key_rows = lax.dynamic_slice_in_dim(everything, key_first, window_rows, 0)
    queries = mla_query.reshape(slab_rows, head_count, NOPE + ROPE)
    score_scale = 1.0 / math.sqrt(NOPE + ROPE)
    key_places = key_first + jnp.arange(window_rows, dtype=jnp.int32)
    key_docs = doc_of(key_places, doc_starts)
    allowed = (key_places[None, :] <= positions[:, None]) & (
        key_docs[None, :] == docids[:, None]
    )
    allowed_flags = allowed.astype(jnp.int32)
    value_width = value_up.shape[1] // head_count
    group_count = carry_rounds(slab_rows)
    while head_count % group_count:
        group_count -= 1
    per_group = head_count // group_count

    def attend_group(group, tie):
        rows, _ = lax.optimization_barrier((key_rows, tie))
        heads = slice(group * per_group, (group + 1) * per_group)
        latent_part = rows[:, :LATENT]
        keys_nope = (
            jnp.dot(
                latent_part,
                key_up[:, group * per_group * NOPE : (group + 1) * per_group * NOPE],
                preferred_element_type=jnp.float32,
            )
            .astype(jnp.bfloat16)
            .reshape(window_rows, per_group, NOPE)
        )
        values = (
            jnp.dot(
                latent_part,
                value_up[
                    :, group * per_group * value_width : (group + 1) * per_group * value_width
                ],
                preferred_element_type=jnp.float32,
            )
            .astype(jnp.bfloat16)
            .reshape(window_rows, per_group, value_width)
        )
        return attend_kernel(
            jnp.transpose(queries[:, heads, :NOPE], (1, 0, 2)),
            jnp.transpose(queries[:, heads, NOPE:], (1, 0, 2)),
            keys_nope.reshape(window_rows, -1),
            rows[:, LATENT:],
            values.reshape(window_rows, -1),
            allowed_flags,
            score_scale,
        )

    def latents_ready(value):
        return lax.optimization_barrier((key_rows, value))[1]

    return attend_group, group_count, latents_ready


def solution(mesh):
    in_specs = (
        P(("batch", "ctx"), None),
        P(("batch", "ctx"), None),
        P(("batch", "ctx"), None),
        P(("batch", "ctx"), None),
        P(("batch", "ctx"), None),
        P(("batch", "ctx"), None),
        P(("batch", "ctx"), None),
        P(),
        P(),
        P("batch"),
    )
    out_specs = (P(("batch", "ctx"), None), P(("batch", "ctx"), None))
    return jax.shard_map(local, mesh=mesh, in_specs=in_specs, out_specs=out_specs, check_vma=False)
```

```python
import math

import jax
import jax.numpy as jnp
from jax import lax
from jax.sharding import PartitionSpec as P

NOPE = 128
ROPE = 64
LATENT = 512
BLOCK = 64


PRECISE_PRODUCT = lax.Precision.HIGHEST


def prefix(array, axis, join, neutral):
    place = lax.axis_index(axis)
    gathered = jax.tree.map(
        lambda a, kind: lax.all_gather(a.astype(kind), axis),
        array,
        jax.tree.map(lambda a: jnp.bfloat16 if a.dtype == jnp.float32 else a.dtype, array),
    )
    state = jax.tree.map(lambda a, e: jnp.zeros_like(a) + jnp.asarray(e, a.dtype), array, neutral)

    def one(step, state):
        return join(
            state,
            jax.tree.map(
                lambda a, own: lax.dynamic_index_in_dim(a, step, 0, False).astype(own.dtype),
                gathered,
                array,
            ),
        )

    return lax.fori_loop(0, place, one, state)


def shifted(block, axis, distance):
    devices = range(lax.axis_size(axis))
    route = [(i - distance, i) for i in devices if i - distance in devices]
    return lax.ppermute(block, axis, route)


def unit_rows(values):
    return values * lax.rsqrt(jnp.sum(values * values, axis=-1, keepdims=True) + 1e-06)


def doc_of(positions, doc_starts):
    match_count = (doc_starts[None, :] <= positions[:, None]).astype(jnp.int32)
    return jnp.sum(match_count, axis=1) - 1


def unit_lower_inverse(strictly_lower):
    length = strictly_lower.shape[-1]
    identity = jnp.eye(length, dtype=jnp.float32)[None]
    result = identity - strictly_lower
    power_term = strictly_lower
    for level_index in range(length.bit_length() - 2):
        power_term = jnp.einsum("hij,hjk->hik", power_term, power_term, precision=PRECISE_PRODUCT)
        result = jnp.einsum(
            "hij,hjk->hik", result, identity + power_term, precision=PRECISE_PRODUCT
        )
    return result


def block_terms(query_unit, keyvec, valvec, logarithm_decay, write_gain, docids, prevdoc):
    length = docids.shape[0]
    cumulative = jnp.cumsum(logarithm_decay, axis=0)
    growth = jnp.exp(cumulative)
    key_plus = keyvec * growth
    key_minus = keyvec * jnp.exp(-cumulative)
    query_plus = query_unit * growth
    places = jnp.arange(length)
    same_doc = docids[:, None] == docids[None, :]
    strict = (places[:, None] > places[None, :]) & same_doc
    causal = (places[:, None] >= places[None, :]) & same_doc
    follow = (docids == prevdoc).astype(jnp.float32)
    inner_prod = jnp.einsum("thk,shk->hts", key_plus, key_minus, precision=PRECISE_PRODUCT)
    strictly_lower = (
        jnp.where(strict[None], inner_prod, 0.0) * jnp.transpose(write_gain)[:, :, None]
    )
    inverse = unit_lower_inverse(strictly_lower)
    value_rhs = jnp.transpose(valvec * write_gain[:, :, None], (1, 0, 2))
    key_rhs = jnp.transpose(key_plus * (write_gain * follow[:, None])[:, :, None], (1, 0, 2))
    value_solution = jnp.einsum("hts,hsv->htv", inverse, value_rhs, precision=PRECISE_PRODUCT)
    solved_key = jnp.einsum("hts,hsk->htk", inverse, key_rhs, precision=PRECISE_PRODUCT)
    mixing = jnp.where(
        causal[None],
        jnp.einsum("thk,shk->hts", query_plus, key_minus, precision=PRECISE_PRODUCT),
        0.0,
    )
    local_output = jnp.einsum("hts,hsv->htv", mixing, value_solution, precision=PRECISE_PRODUCT)
    query_effective = jnp.transpose(query_plus * follow[:, None, None], (1, 0, 2)) - jnp.einsum(
        "hts,hsk->htk", mixing, solved_key, precision=PRECISE_PRODUCT
    )
    last_doc = (docids == docids[length - 1]).astype(jnp.float32)
    key_trailing = (
        keyvec * jnp.exp(cumulative[length - 1][None] - cumulative) * last_doc[:, None, None]
    )
    growth_last = growth[length - 1]
    diagonal_map = growth_last[:, :, None] * jnp.eye(keyvec.shape[2], dtype=jnp.float32)[None]
    handed_operator = follow[length - 1] * diagonal_map - jnp.einsum(
        "shk,hsj->hkj", key_trailing, solved_key, precision=PRECISE_PRODUCT
    )
    handed_update = jnp.einsum(
        "omt,mor->mtr", key_trailing, value_solution, precision=PRECISE_PRODUCT
    )
    return (local_output, query_effective, handed_operator, handed_update)


def compose(prior_slab, successor_slab):
    joined_map = jnp.einsum(
        "hkj,hjl->hkl", successor_slab[0], prior_slab[0], precision=PRECISE_PRODUCT
    )
    combined_increment = (
        jnp.einsum("ytn,yne->yte", successor_slab[0], prior_slab[1], precision=PRECISE_PRODUCT)
        + successor_slab[1]
    )
    return (joined_map, combined_increment)


def local(
    kda_query,
    kda_key,
    kda_value,
    log_decay,
    write_rate,
    mla_query,
    latents,
    key_up,
    value_up,
    doc_lengths,
):
    slab_rows = latents.shape[0]
    head_count = write_rate.shape[1]
    first_row = lax.axis_index("ctx") * slab_rows
    doc_starts = jnp.cumsum(doc_lengths) - doc_lengths
    positions = first_row + jnp.arange(slab_rows, dtype=jnp.int32)
    docids = doc_of(positions, doc_starts)
    query_unit = unit_rows(kda_query.astype(jnp.float32).reshape(slab_rows, head_count, -1))
    keyvec = unit_rows(kda_key.astype(jnp.float32).reshape(slab_rows, head_count, -1))
    valvec = kda_value.astype(jnp.float32).reshape(slab_rows, head_count, -1)
    logarithm_decay = log_decay.astype(jnp.float32).reshape(slab_rows, head_count, -1)
    block_count = slab_rows // BLOCK
    prevdocs = doc_of(first_row + jnp.arange(block_count, dtype=jnp.int32) * BLOCK - 1, doc_starts)

    def shaped(values):
        return values.reshape((block_count, BLOCK) + values.shape[1:])

    block_outs = jax.vmap(block_terms)(
        shaped(query_unit),
        shaped(keyvec),
        shaped(valvec),
        shaped(logarithm_decay),
        shaped(write_rate),
        shaped(docids),
        prevdocs,
    )
    key_dim = keyvec.shape[2]
    value_dim = valvec.shape[2]
    identity_map = jnp.broadcast_to(
        jnp.eye(key_dim, dtype=jnp.float32)[None], (head_count, key_dim, key_dim)
    )
    zero_add = jnp.zeros((head_count, key_dim, value_dim), jnp.float32)

    def advance_block(prefix_pair, block_item):
        map_before, update_from_prior = prefix_pair
        local_output, query_effective, handed_operator, handed_update = block_item
        eff_now = jnp.einsum("htk,hkj->htj", query_effective, map_before, precision=PRECISE_PRODUCT)
        output_current = local_output + jnp.einsum(
            "cor,crm->com", query_effective, update_from_prior, precision=PRECISE_PRODUCT
        )
        map_after = jnp.einsum(
            "hkj,hjl->hkl", handed_operator, map_before, precision=PRECISE_PRODUCT
        )
        increment_later = (
            jnp.einsum(
                "ytn,yne->yte", handed_operator, update_from_prior, precision=PRECISE_PRODUCT
            )
            + handed_update
        )
        return ((map_after, increment_later), (eff_now, output_current))

    local_output, query_effective, handed_operator, handed_update = block_outs
    slab_pair = (handed_operator[0], handed_update[0])
    effective_blocks, output_blocks = [query_effective[0]], [local_output[0]]
    for block in range(1, block_count):
        slab_pair, (eff_now, output_current) = advance_block(
            slab_pair,
            (local_output[block], query_effective[block], handed_operator[block], handed_update[block]),
        )
        effective_blocks.append(eff_now)
        output_blocks.append(output_current)
    effective_everything = jnp.stack(effective_blocks)
    output_everything = jnp.stack(output_blocks)
    attend_group, group_count = latent_attention(
        mla_query, latents, key_up, value_up, positions, docids, doc_starts, head_count
    )
    carried_in, mla_parts = incoming_state(slab_pair, slab_rows, attend_group, group_count)
    delta_attention_complete = output_everything + jnp.einsum(
        "enzx,nxu->enzu", effective_everything, carried_in, precision=lax.Precision.HIGH
    )
    kda_out = (
        jnp.transpose(delta_attention_complete, (0, 2, 1, 3))
        .reshape(slab_rows, -1)
        .astype(jnp.bfloat16)
    )
    mla_out = jnp.concatenate(mla_parts, axis=1).reshape(slab_rows, -1)
    return (kda_out, mla_out)


def window_slabs_of(slab_rows):
    longest = lax.axis_size("ctx") * slab_rows // 2
    return -(-longest // slab_rows)


def carry_rounds(slab_rows):
    window = window_slabs_of(slab_rows)
    distance, rounds = 1, 2
    while 2 * distance < window:
        distance, rounds = 2 * distance, rounds + 1
    return rounds


def incoming_state(slab_pair, slab_rows, attend_group, group_count):
    map_now, add_now = slab_pair
    window = window_slabs_of(slab_rows)
    rounds = carry_rounds(slab_rows)
    groups_at = [[] for _ in range(rounds)]
    for group in range(group_count):
        groups_at[rounds - group_count + group if rounds > group_count else group * rounds // group_count].append(group)
    parts = []

    def exchange(value, distance, step):
        sent = lax.optimization_barrier(value.astype(jnp.bfloat16))
        got = shifted(sent, "ctx", distance)
        done = [attend_group(group, sent) for group in groups_at[step]]
        got, done = lax.optimization_barrier((got, done))
        parts.extend(done)
        return got.astype(jnp.float32)

    def product(left, right):
        return jnp.einsum("hkj,hjl->hkl", left, right, precision=lax.Precision.HIGH)

    value_dim = add_now.shape[2]
    distance, step = 1, 0
    while 2 * distance < window:
        before = exchange(jnp.concatenate([add_now, map_now], axis=2), distance, step)
        joined = product(map_now, before)
        add_now = joined[:, :, :value_dim] + add_now
        map_now = joined[:, :, value_dim:]
        distance, step = 2 * distance, step + 1
    add_now = product(map_now, exchange(add_now, distance, step)) + add_now
    return exchange(add_now, 1, step + 1), parts


def latent_attention(
    mla_query, latents, key_up, value_up, positions, docids, doc_starts, head_count
):
    slab_rows = latents.shape[0]
    slabs = lax.axis_size("ctx")
    reach = window_slabs_of(slab_rows)
    window_slabs = min(reach + 1, slabs)
    window_rows = window_slabs * slab_rows
    everything = lax.all_gather(latents, "ctx", tiled=True)
    first_slab = jnp.clip(lax.axis_index("ctx") - reach, 0, slabs - window_slabs)
    key_first = first_slab * slab_rows
    key_rows = lax.dynamic_slice_in_dim(everything, key_first, window_rows, 0)
    queries = mla_query.reshape(slab_rows, head_count, NOPE + ROPE)
    score_scale = 1.0 / math.sqrt(NOPE + ROPE)
    key_places = key_first + jnp.arange(window_rows, dtype=jnp.int32)
    key_docs = doc_of(key_places, doc_starts)
    allowed = (key_places[None, :] <= positions[:, None]) & (
        key_docs[None, :] == docids[:, None]
    )
    value_width = value_up.shape[1] // head_count
    group_count = carry_rounds(slab_rows)
    while head_count % group_count:
        group_count -= 1
    per_group = head_count // group_count

    def attend_group(group, tie):
        rows, _ = lax.optimization_barrier((key_rows, tie))
        heads = slice(group * per_group, (group + 1) * per_group)
        latent_part = rows[:, :LATENT]
        keys_nope = (
            jnp.dot(
                latent_part,
                key_up[:, group * per_group * NOPE : (group + 1) * per_group * NOPE],
                preferred_element_type=jnp.float32,
            )
            .astype(jnp.bfloat16)
            .reshape(window_rows, per_group, NOPE)
        )
        values = (
            jnp.dot(
                latent_part,
                value_up[
                    :, group * per_group * value_width : (group + 1) * per_group * value_width
                ],
                preferred_element_type=jnp.float32,
            )
            .astype(jnp.bfloat16)
            .reshape(window_rows, per_group, value_width)
        )
        scores = jnp.einsum(
            "thd,shd->hts",
            queries[:, heads, :NOPE],
            keys_nope,
            preferred_element_type=jnp.float32,
        )
        scores = (
            scores
            + jnp.einsum(
                "thr,sr->hts",
                queries[:, heads, NOPE:],
                rows[:, LATENT:],
                preferred_element_type=jnp.float32,
            )
        ) * score_scale
        masked = jnp.where(allowed[None], scores, -1e30)
        row_max = jnp.max(masked, axis=2, keepdims=True)
        weights = jnp.where(allowed[None], jnp.exp(masked - row_max), 0.0)
        row_total = jnp.sum(weights, axis=2)
        summed = jnp.einsum(
            "hts,shv->thv",
            weights.astype(jnp.bfloat16),
            values,
            preferred_element_type=jnp.float32,
        )
        return (summed / jnp.transpose(row_total)[:, :, None]).astype(jnp.bfloat16)

    return attend_group, group_count


def solution(mesh):
    in_specs = (
        P(("batch", "ctx"), None),
        P(("batch", "ctx"), None),
        P(("batch", "ctx"), None),
        P(("batch", "ctx"), None),
        P(("batch", "ctx"), None),
        P(("batch", "ctx"), None),
        P(("batch", "ctx"), None),
        P(),
        P(),
        P("batch"),
    )
    out_specs = (P(("batch", "ctx"), None), P(("batch", "ctx"), None))
    return jax.shard_map(local, mesh=mesh, in_specs=in_specs, out_specs=out_specs, check_vma=False)
```

```python
import math

import jax
import jax.numpy as jnp
from jax import lax
from jax.sharding import PartitionSpec as P

NOPE = 128
ROPE = 64
LATENT = 512
BLOCK = 64


PRECISE_PRODUCT = lax.Precision.HIGHEST


def prefix(array, axis, join, neutral):
    place = lax.axis_index(axis)
    gathered = jax.tree.map(
        lambda a, kind: lax.all_gather(a.astype(kind), axis),
        array,
        jax.tree.map(lambda a: jnp.bfloat16 if a.dtype == jnp.float32 else a.dtype, array),
    )
    state = jax.tree.map(lambda a, e: jnp.zeros_like(a) + jnp.asarray(e, a.dtype), array, neutral)

    def one(step, state):
        return join(
            state,
            jax.tree.map(
                lambda a, own: lax.dynamic_index_in_dim(a, step, 0, False).astype(own.dtype),
                gathered,
                array,
            ),
        )

    return lax.fori_loop(0, place, one, state)


def shifted(block, axis, distance):
    devices = range(lax.axis_size(axis))
    route = [(i - distance, i) for i in devices if i - distance in devices]
    return lax.ppermute(block, axis, route)


def unit_rows(values):
    return values * lax.rsqrt(jnp.sum(values * values, axis=-1, keepdims=True) + 1e-06)


def doc_of(positions, doc_starts):
    match_count = (doc_starts[None, :] <= positions[:, None]).astype(jnp.int32)
    return jnp.sum(match_count, axis=1) - 1


def unit_lower_inverse(strictly_lower):
    length = strictly_lower.shape[-1]
    identity = jnp.eye(length, dtype=jnp.float32)[None]
    result = identity - strictly_lower
    power_term = strictly_lower
    for level_index in range(length.bit_length() - 2):
        power_term = jnp.einsum("hij,hjk->hik", power_term, power_term, precision=PRECISE_PRODUCT)
        result = jnp.einsum(
            "hij,hjk->hik", result, identity + power_term, precision=PRECISE_PRODUCT
        )
    return result


def block_terms(query_unit, keyvec, valvec, logarithm_decay, write_gain, docids, prevdoc):
    length = docids.shape[0]
    cumulative = jnp.cumsum(logarithm_decay, axis=0)
    growth = jnp.exp(cumulative)
    key_plus = keyvec * growth
    key_minus = keyvec * jnp.exp(-cumulative)
    query_plus = query_unit * growth
    places = jnp.arange(length)
    same_doc = docids[:, None] == docids[None, :]
    strict = (places[:, None] > places[None, :]) & same_doc
    causal = (places[:, None] >= places[None, :]) & same_doc
    follow = (docids == prevdoc).astype(jnp.float32)
    inner_prod = jnp.einsum("thk,shk->hts", key_plus, key_minus, precision=PRECISE_PRODUCT)
    strictly_lower = (
        jnp.where(strict[None], inner_prod, 0.0) * jnp.transpose(write_gain)[:, :, None]
    )
    inverse = unit_lower_inverse(strictly_lower)
    value_rhs = jnp.transpose(valvec * write_gain[:, :, None], (1, 0, 2))
    key_rhs = jnp.transpose(key_plus * (write_gain * follow[:, None])[:, :, None], (1, 0, 2))
    value_solution = jnp.einsum("hts,hsv->htv", inverse, value_rhs, precision=PRECISE_PRODUCT)
    solved_key = jnp.einsum("hts,hsk->htk", inverse, key_rhs, precision=PRECISE_PRODUCT)
    mixing = jnp.where(
        causal[None],
        jnp.einsum("thk,shk->hts", query_plus, key_minus, precision=PRECISE_PRODUCT),
        0.0,
    )
    local_output = jnp.einsum("hts,hsv->htv", mixing, value_solution, precision=PRECISE_PRODUCT)
    query_effective = jnp.transpose(query_plus * follow[:, None, None], (1, 0, 2)) - jnp.einsum(
        "hts,hsk->htk", mixing, solved_key, precision=PRECISE_PRODUCT
    )
    last_doc = (docids == docids[length - 1]).astype(jnp.float32)
    key_trailing = (
        keyvec * jnp.exp(cumulative[length - 1][None] - cumulative) * last_doc[:, None, None]
    )
    growth_last = growth[length - 1]
    diagonal_map = growth_last[:, :, None] * jnp.eye(keyvec.shape[2], dtype=jnp.float32)[None]
    handed_operator = follow[length - 1] * diagonal_map - jnp.einsum(
        "shk,hsj->hkj", key_trailing, solved_key, precision=PRECISE_PRODUCT
    )
    handed_update = jnp.einsum(
        "omt,mor->mtr", key_trailing, value_solution, precision=PRECISE_PRODUCT
    )
    return (local_output, query_effective, handed_operator, handed_update)


def compose(prior_slab, successor_slab):
    joined_map = jnp.einsum(
        "hkj,hjl->hkl", successor_slab[0], prior_slab[0], precision=PRECISE_PRODUCT
    )
    combined_increment = (
        jnp.einsum("ytn,yne->yte", successor_slab[0], prior_slab[1], precision=PRECISE_PRODUCT)
        + successor_slab[1]
    )
    return (joined_map, combined_increment)


def local(
    kda_query,
    kda_key,
    kda_value,
    log_decay,
    write_rate,
    mla_query,
    latents,
    key_up,
    value_up,
    doc_lengths,
):
    slab_rows = latents.shape[0]
    head_count = write_rate.shape[1]
    first_row = lax.axis_index("ctx") * slab_rows
    doc_starts = jnp.cumsum(doc_lengths) - doc_lengths
    positions = first_row + jnp.arange(slab_rows, dtype=jnp.int32)
    docids = doc_of(positions, doc_starts)
    query_unit = unit_rows(kda_query.astype(jnp.float32).reshape(slab_rows, head_count, -1))
    keyvec = unit_rows(kda_key.astype(jnp.float32).reshape(slab_rows, head_count, -1))
    valvec = kda_value.astype(jnp.float32).reshape(slab_rows, head_count, -1)
    logarithm_decay = log_decay.astype(jnp.float32).reshape(slab_rows, head_count, -1)
    block_count = slab_rows // BLOCK
    prevdocs = doc_of(first_row + jnp.arange(block_count, dtype=jnp.int32) * BLOCK - 1, doc_starts)

    def shaped(values):
        return values.reshape((block_count, BLOCK) + values.shape[1:])

    block_outs = jax.vmap(block_terms)(
        shaped(query_unit),
        shaped(keyvec),
        shaped(valvec),
        shaped(logarithm_decay),
        shaped(write_rate),
        shaped(docids),
        prevdocs,
    )
    key_dim = keyvec.shape[2]
    value_dim = valvec.shape[2]
    identity_map = jnp.broadcast_to(
        jnp.eye(key_dim, dtype=jnp.float32)[None], (head_count, key_dim, key_dim)
    )
    zero_add = jnp.zeros((head_count, key_dim, value_dim), jnp.float32)

    def advance_block(prefix_pair, block_item):
        map_before, update_from_prior = prefix_pair
        local_output, query_effective, handed_operator, handed_update = block_item
        eff_now = jnp.einsum("htk,hkj->htj", query_effective, map_before, precision=PRECISE_PRODUCT)
        output_current = local_output + jnp.einsum(
            "cor,crm->com", query_effective, update_from_prior, precision=PRECISE_PRODUCT
        )
        map_after = jnp.einsum(
            "hkj,hjl->hkl", handed_operator, map_before, precision=PRECISE_PRODUCT
        )
        increment_later = (
            jnp.einsum(
                "ytn,yne->yte", handed_operator, update_from_prior, precision=PRECISE_PRODUCT
            )
            + handed_update
        )
        return ((map_after, increment_later), (eff_now, output_current))

    local_output, query_effective, handed_operator, handed_update = block_outs
    slab_pair = (handed_operator[0], handed_update[0])
    effective_blocks, output_blocks = [query_effective[0]], [local_output[0]]
    for block in range(1, block_count):
        slab_pair, (eff_now, output_current) = advance_block(
            slab_pair,
            (local_output[block], query_effective[block], handed_operator[block], handed_update[block]),
        )
        effective_blocks.append(eff_now)
        output_blocks.append(output_current)
    effective_everything = jnp.stack(effective_blocks)
    output_everything = jnp.stack(output_blocks)
    attend_group, group_count = latent_attention(
        mla_query, latents, key_up, value_up, positions, docids, doc_starts, head_count
    )
    carried_in, mla_parts = incoming_state(slab_pair, slab_rows, attend_group, group_count)
    delta_attention_complete = output_everything + jnp.einsum(
        "enzx,nxu->enzu", effective_everything, carried_in, precision=PRECISE_PRODUCT
    )
    kda_out = (
        jnp.transpose(delta_attention_complete, (0, 2, 1, 3))
        .reshape(slab_rows, -1)
        .astype(jnp.bfloat16)
    )
    mla_out = jnp.concatenate(mla_parts, axis=1).reshape(slab_rows, -1)
    return (kda_out, mla_out)


def window_slabs_of(slab_rows):
    longest = lax.axis_size("ctx") * slab_rows // 2
    return -(-longest // slab_rows)


def carry_rounds(slab_rows):
    window = window_slabs_of(slab_rows)
    distance, rounds = 1, 2
    while 2 * distance < window:
        distance, rounds = 2 * distance, rounds + 1
    return rounds


def incoming_state(slab_pair, slab_rows, attend_group, group_count):
    map_now, add_now = slab_pair
    window = window_slabs_of(slab_rows)
    rounds = carry_rounds(slab_rows)
    groups_at = [[] for _ in range(rounds)]
    for group in range(group_count):
        groups_at[rounds - group_count + group if rounds > group_count else group * rounds // group_count].append(group)
    parts = []

    def exchange(value, distance, step):
        sent = lax.optimization_barrier(value.astype(jnp.bfloat16))
        got = shifted(sent, "ctx", distance)
        done = [attend_group(group, sent) for group in groups_at[step]]
        got, done = lax.optimization_barrier((got, done))
        parts.extend(done)
        return got.astype(jnp.float32)

    def product(left, right):
        return jnp.einsum("hkj,hjl->hkl", left, right, precision=PRECISE_PRODUCT)

    value_dim = add_now.shape[2]
    distance, step = 1, 0
    while 2 * distance < window:
        before = exchange(jnp.concatenate([add_now, map_now], axis=2), distance, step)
        joined = product(map_now, before)
        add_now = joined[:, :, :value_dim] + add_now
        map_now = joined[:, :, value_dim:]
        distance, step = 2 * distance, step + 1
    add_now = product(map_now, exchange(add_now, distance, step)) + add_now
    return exchange(add_now, 1, step + 1), parts


def latent_attention(
    mla_query, latents, key_up, value_up, positions, docids, doc_starts, head_count
):
    slab_rows = latents.shape[0]
    slabs = lax.axis_size("ctx")
    reach = window_slabs_of(slab_rows)
    window_slabs = min(reach + 1, slabs)
    window_rows = window_slabs * slab_rows
    everything = lax.all_gather(latents, "ctx", tiled=True)
    first_slab = jnp.clip(lax.axis_index("ctx") - reach, 0, slabs - window_slabs)
    key_first = first_slab * slab_rows
    key_rows = lax.dynamic_slice_in_dim(everything, key_first, window_rows, 0)
    queries = mla_query.reshape(slab_rows, head_count, NOPE + ROPE)
    score_scale = 1.0 / math.sqrt(NOPE + ROPE)
    key_places = key_first + jnp.arange(window_rows, dtype=jnp.int32)
    key_docs = doc_of(key_places, doc_starts)
    allowed = (key_places[None, :] <= positions[:, None]) & (
        key_docs[None, :] == docids[:, None]
    )
    value_width = value_up.shape[1] // head_count
    group_count = carry_rounds(slab_rows)
    while head_count % group_count:
        group_count -= 1
    per_group = head_count // group_count

    def attend_group(group, tie):
        rows, _ = lax.optimization_barrier((key_rows, tie))
        heads = slice(group * per_group, (group + 1) * per_group)
        latent_part = rows[:, :LATENT]
        keys_nope = jnp.einsum(
            "sl,lhd->hsd",
            latent_part,
            key_up[:, group * per_group * NOPE : (group + 1) * per_group * NOPE].reshape(
                LATENT, per_group, NOPE
            ),
            preferred_element_type=jnp.float32,
        ).astype(jnp.bfloat16)
        values = jnp.einsum(
            "sl,lhv->hsv",
            latent_part,
            value_up[
                :, group * per_group * value_width : (group + 1) * per_group * value_width
            ].reshape(LATENT, per_group, value_width),
            preferred_element_type=jnp.float32,
        ).astype(jnp.bfloat16)
        scores = jnp.einsum(
            "thd,hsd->hts",
            queries[:, heads, :NOPE],
            keys_nope,
            preferred_element_type=jnp.float32,
        )
        scores = (
            scores
            + jnp.einsum(
                "thr,sr->hts",
                queries[:, heads, NOPE:],
                rows[:, LATENT:],
                preferred_element_type=jnp.float32,
            )
        ) * score_scale
        masked = jnp.where(allowed[None], scores, -1e30)
        row_max = jnp.max(masked, axis=2, keepdims=True)
        weights = jnp.where(allowed[None], jnp.exp(masked - row_max), 0.0)
        row_total = jnp.sum(weights, axis=2)
        summed = jnp.einsum(
            "hts,hsv->thv",
            weights.astype(jnp.bfloat16),
            values,
            preferred_element_type=jnp.float32,
        )
        return (summed / jnp.transpose(row_total)[:, :, None]).astype(jnp.bfloat16)

    return attend_group, group_count


def solution(mesh):
    in_specs = (
        P(("batch", "ctx"), None),
        P(("batch", "ctx"), None),
        P(("batch", "ctx"), None),
        P(("batch", "ctx"), None),
        P(("batch", "ctx"), None),
        P(("batch", "ctx"), None),
        P(("batch", "ctx"), None),
        P(),
        P(),
        P("batch"),
    )
    out_specs = (P(("batch", "ctx"), None), P(("batch", "ctx"), None))
    return jax.shard_map(local, mesh=mesh, in_specs=in_specs, out_specs=out_specs, check_vma=False)
```

```python
import math

import jax
import jax.numpy as jnp
from jax import lax
from jax.sharding import PartitionSpec as P

NOPE = 128
ROPE = 64
LATENT = 512
BLOCK = 64


PRECISE_PRODUCT = lax.Precision.HIGHEST


def prefix(array, axis, join, neutral):
    place = lax.axis_index(axis)
    gathered = jax.tree.map(
        lambda a, kind: lax.all_gather(a.astype(kind), axis),
        array,
        jax.tree.map(lambda a: jnp.bfloat16 if a.dtype == jnp.float32 else a.dtype, array),
    )
    state = jax.tree.map(lambda a, e: jnp.zeros_like(a) + jnp.asarray(e, a.dtype), array, neutral)

    def one(step, state):
        return join(
            state,
            jax.tree.map(
                lambda a, own: lax.dynamic_index_in_dim(a, step, 0, False).astype(own.dtype),
                gathered,
                array,
            ),
        )

    return lax.fori_loop(0, place, one, state)


def shifted(block, axis, distance):
    devices = range(lax.axis_size(axis))
    route = [(i - distance, i) for i in devices if i - distance in devices]
    return lax.ppermute(block, axis, route)


def unit_rows(values):
    return values * lax.rsqrt(jnp.sum(values * values, axis=-1, keepdims=True) + 1e-06)


def doc_of(positions, doc_starts):
    match_count = (doc_starts[None, :] <= positions[:, None]).astype(jnp.int32)
    return jnp.sum(match_count, axis=1) - 1


def unit_lower_inverse(strictly_lower):
    length = strictly_lower.shape[-1]
    identity = jnp.eye(length, dtype=jnp.float32)[None]
    result = identity - strictly_lower
    power_term = strictly_lower
    for level_index in range(length.bit_length() - 2):
        power_term = jnp.einsum("hij,hjk->hik", power_term, power_term, precision=PRECISE_PRODUCT)
        result = result + jnp.einsum(
            "hij,hjk->hik", result, power_term, precision=PRECISE_PRODUCT
        )
    return result


def block_terms(query_unit, keyvec, valvec, logarithm_decay, write_gain, docids, prevdoc):
    length = docids.shape[0]
    cumulative = jnp.cumsum(logarithm_decay, axis=0)
    growth = jnp.exp(cumulative)
    key_plus = keyvec * growth
    key_minus = keyvec * jnp.exp(-cumulative)
    query_plus = query_unit * growth
    places = jnp.arange(length)
    same_doc = docids[:, None] == docids[None, :]
    strict = (places[:, None] > places[None, :]) & same_doc
    causal = (places[:, None] >= places[None, :]) & same_doc
    follow = (docids == prevdoc).astype(jnp.float32)
    inner_prod = jnp.einsum("thk,shk->hts", key_plus, key_minus, precision=PRECISE_PRODUCT)
    strictly_lower = (
        jnp.where(strict[None], inner_prod, 0.0) * jnp.transpose(write_gain)[:, :, None]
    )
    inverse = unit_lower_inverse(strictly_lower)
    value_rhs = jnp.transpose(valvec * write_gain[:, :, None], (1, 0, 2))
    key_rhs = jnp.transpose(key_plus * (write_gain * follow[:, None])[:, :, None], (1, 0, 2))
    value_solution = jnp.einsum("hts,hsv->htv", inverse, value_rhs, precision=PRECISE_PRODUCT)
    solved_key = jnp.einsum("hts,hsk->htk", inverse, key_rhs, precision=PRECISE_PRODUCT)
    mixing = jnp.where(
        causal[None],
        jnp.einsum("thk,shk->hts", query_plus, key_minus, precision=PRECISE_PRODUCT),
        0.0,
    )
    local_output = jnp.einsum("hts,hsv->htv", mixing, value_solution, precision=PRECISE_PRODUCT)
    query_effective = jnp.transpose(query_plus * follow[:, None, None], (1, 0, 2)) - jnp.einsum(
        "hts,hsk->htk", mixing, solved_key, precision=PRECISE_PRODUCT
    )
    last_doc = (docids == docids[length - 1]).astype(jnp.float32)
    key_trailing = (
        keyvec * jnp.exp(cumulative[length - 1][None] - cumulative) * last_doc[:, None, None]
    )
    growth_last = growth[length - 1]
    diagonal_map = growth_last[:, :, None] * jnp.eye(keyvec.shape[2], dtype=jnp.float32)[None]
    handed_operator = follow[length - 1] * diagonal_map - jnp.einsum(
        "shk,hsj->hkj", key_trailing, solved_key, precision=PRECISE_PRODUCT
    )
    handed_update = jnp.einsum(
        "omt,mor->mtr", key_trailing, value_solution, precision=PRECISE_PRODUCT
    )
    return (local_output, query_effective, handed_operator, handed_update)


def compose(prior_slab, successor_slab):
    joined_map = jnp.einsum(
        "hkj,hjl->hkl", successor_slab[0], prior_slab[0], precision=PRECISE_PRODUCT
    )
    combined_increment = (
        jnp.einsum("ytn,yne->yte", successor_slab[0], prior_slab[1], precision=PRECISE_PRODUCT)
        + successor_slab[1]
    )
    return (joined_map, combined_increment)


def local(
    kda_query,
    kda_key,
    kda_value,
    log_decay,
    write_rate,
    mla_query,
    latents,
    key_up,
    value_up,
    doc_lengths,
):
    slab_rows = latents.shape[0]
    head_count = write_rate.shape[1]
    first_row = lax.axis_index("ctx") * slab_rows
    doc_starts = jnp.cumsum(doc_lengths) - doc_lengths
    positions = first_row + jnp.arange(slab_rows, dtype=jnp.int32)
    docids = doc_of(positions, doc_starts)
    query_unit = unit_rows(kda_query.astype(jnp.float32).reshape(slab_rows, head_count, -1))
    keyvec = unit_rows(kda_key.astype(jnp.float32).reshape(slab_rows, head_count, -1))
    valvec = kda_value.astype(jnp.float32).reshape(slab_rows, head_count, -1)
    logarithm_decay = log_decay.astype(jnp.float32).reshape(slab_rows, head_count, -1)
    block_count = slab_rows // BLOCK
    prevdocs = doc_of(first_row + jnp.arange(block_count, dtype=jnp.int32) * BLOCK - 1, doc_starts)

    def shaped(values):
        return values.reshape((block_count, BLOCK) + values.shape[1:])

    block_outs = jax.vmap(block_terms)(
        shaped(query_unit),
        shaped(keyvec),
        shaped(valvec),
        shaped(logarithm_decay),
        shaped(write_rate),
        shaped(docids),
        prevdocs,
    )
    key_dim = keyvec.shape[2]
    value_dim = valvec.shape[2]
    identity_map = jnp.broadcast_to(
        jnp.eye(key_dim, dtype=jnp.float32)[None], (head_count, key_dim, key_dim)
    )
    zero_add = jnp.zeros((head_count, key_dim, value_dim), jnp.float32)

    def advance_block(prefix_pair, block_item):
        map_before, update_from_prior = prefix_pair
        local_output, query_effective, handed_operator, handed_update = block_item
        eff_now = jnp.einsum("htk,hkj->htj", query_effective, map_before, precision=PRECISE_PRODUCT)
        output_current = local_output + jnp.einsum(
            "cor,crm->com", query_effective, update_from_prior, precision=PRECISE_PRODUCT
        )
        map_after = jnp.einsum(
            "hkj,hjl->hkl", handed_operator, map_before, precision=PRECISE_PRODUCT
        )
        increment_later = (
            jnp.einsum(
                "ytn,yne->yte", handed_operator, update_from_prior, precision=PRECISE_PRODUCT
            )
            + handed_update
        )
        return ((map_after, increment_later), (eff_now, output_current))

    local_output, query_effective, handed_operator, handed_update = block_outs
    slab_pair = (handed_operator[0], handed_update[0])
    effective_blocks, output_blocks = [query_effective[0]], [local_output[0]]
    for block in range(1, block_count):
        slab_pair, (eff_now, output_current) = advance_block(
            slab_pair,
            (local_output[block], query_effective[block], handed_operator[block], handed_update[block]),
        )
        effective_blocks.append(eff_now)
        output_blocks.append(output_current)
    effective_everything = jnp.stack(effective_blocks)
    output_everything = jnp.stack(output_blocks)
    attend_group, group_count = latent_attention(
        mla_query, latents, key_up, value_up, positions, docids, doc_starts, head_count
    )
    carried_in, mla_parts = incoming_state(slab_pair, slab_rows, attend_group, group_count)
    delta_attention_complete = output_everything + jnp.einsum(
        "enzx,nxu->enzu", effective_everything, carried_in, precision=PRECISE_PRODUCT
    )
    kda_out = (
        jnp.transpose(delta_attention_complete, (0, 2, 1, 3))
        .reshape(slab_rows, -1)
        .astype(jnp.bfloat16)
    )
    mla_out = jnp.concatenate(mla_parts, axis=1).reshape(slab_rows, -1)
    return (kda_out, mla_out)


def window_slabs_of(slab_rows):
    longest = lax.axis_size("ctx") * slab_rows // 2
    return -(-longest // slab_rows)


def carry_rounds(slab_rows):
    window = window_slabs_of(slab_rows)
    distance, rounds = 1, 2
    while 2 * distance < window:
        distance, rounds = 2 * distance, rounds + 1
    return rounds


def incoming_state(slab_pair, slab_rows, attend_group, group_count):
    map_now, add_now = slab_pair
    window = window_slabs_of(slab_rows)
    rounds = carry_rounds(slab_rows)
    groups_at = [[] for _ in range(rounds)]
    for group in range(group_count):
        groups_at[rounds - group_count + group if rounds > group_count else group * rounds // group_count].append(group)
    parts = []

    def exchange(value, distance, step):
        sent = lax.optimization_barrier(value.astype(jnp.bfloat16))
        got = shifted(sent, "ctx", distance)
        done = [attend_group(group, sent) for group in groups_at[step]]
        got, done = lax.optimization_barrier((got, done))
        parts.extend(done)
        return got.astype(jnp.float32)

    def product(left, right):
        return jnp.einsum("hkj,hjl->hkl", left, right, precision=PRECISE_PRODUCT)

    value_dim = add_now.shape[2]
    distance, step = 1, 0
    while 2 * distance < window:
        before = exchange(jnp.concatenate([add_now, map_now], axis=2), distance, step)
        joined = product(map_now, before)
        add_now = joined[:, :, :value_dim] + add_now
        map_now = joined[:, :, value_dim:]
        distance, step = 2 * distance, step + 1
    add_now = product(map_now, exchange(add_now, distance, step)) + add_now
    return exchange(add_now, 1, step + 1), parts


def latent_attention(
    mla_query, latents, key_up, value_up, positions, docids, doc_starts, head_count
):
    slab_rows = latents.shape[0]
    slabs = lax.axis_size("ctx")
    reach = window_slabs_of(slab_rows)
    window_slabs = min(reach + 1, slabs)
    window_rows = window_slabs * slab_rows
    everything = lax.all_gather(latents, "ctx", tiled=True)
    first_slab = jnp.clip(lax.axis_index("ctx") - reach, 0, slabs - window_slabs)
    key_first = first_slab * slab_rows
    key_rows = lax.dynamic_slice_in_dim(everything, key_first, window_rows, 0)
    queries = mla_query.reshape(slab_rows, head_count, NOPE + ROPE)
    score_scale = 1.0 / math.sqrt(NOPE + ROPE)
    key_places = key_first + jnp.arange(window_rows, dtype=jnp.int32)
    key_docs = doc_of(key_places, doc_starts)
    allowed = (key_places[None, :] <= positions[:, None]) & (
        key_docs[None, :] == docids[:, None]
    )
    value_width = value_up.shape[1] // head_count
    group_count = carry_rounds(slab_rows)
    while head_count % group_count:
        group_count -= 1
    per_group = head_count // group_count

    def attend_group(group, tie):
        rows, _ = lax.optimization_barrier((key_rows, tie))
        heads = slice(group * per_group, (group + 1) * per_group)
        latent_part = rows[:, :LATENT]
        keys_nope = (
            jnp.dot(
                latent_part,
                key_up[:, group * per_group * NOPE : (group + 1) * per_group * NOPE],
                preferred_element_type=jnp.float32,
            )
            .astype(jnp.bfloat16)
            .reshape(window_rows, per_group, NOPE)
        )
        values = (
            jnp.dot(
                latent_part,
                value_up[
                    :, group * per_group * value_width : (group + 1) * per_group * value_width
                ],
                preferred_element_type=jnp.float32,
            )
            .astype(jnp.bfloat16)
            .reshape(window_rows, per_group, value_width)
        )
        scores = jnp.einsum(
            "thd,shd->hts",
            queries[:, heads, :NOPE],
            keys_nope,
            preferred_element_type=jnp.float32,
        )
        scores = (
            scores
            + jnp.einsum(
                "thr,sr->hts",
                queries[:, heads, NOPE:],
                rows[:, LATENT:],
                preferred_element_type=jnp.float32,
            )
        ) * score_scale
        masked = jnp.where(allowed[None], scores, -1e30)
        row_max = jnp.max(masked, axis=2, keepdims=True)
        weights = jnp.where(allowed[None], jnp.exp(masked - row_max), 0.0)
        row_total = jnp.sum(weights, axis=2)
        summed = jnp.einsum(
            "hts,shv->thv",
            weights.astype(jnp.bfloat16),
            values,
            preferred_element_type=jnp.float32,
        )
        return (summed / jnp.transpose(row_total)[:, :, None]).astype(jnp.bfloat16)

    return attend_group, group_count


def solution(mesh):
    in_specs = (
        P(("batch", "ctx"), None),
        P(("batch", "ctx"), None),
        P(("batch", "ctx"), None),
        P(("batch", "ctx"), None),
        P(("batch", "ctx"), None),
        P(("batch", "ctx"), None),
        P(("batch", "ctx"), None),
        P(),
        P(),
        P("batch"),
    )
    out_specs = (P(("batch", "ctx"), None), P(("batch", "ctx"), None))
    return jax.shard_map(local, mesh=mesh, in_specs=in_specs, out_specs=out_specs, check_vma=False)
```
